128 devices in a mesh: circ: 32 (over x_lo, z, y), radax: 4 (over x_hi, core).
Axes of the slice: x: 4 (x_hi: 2, x_lo: 2; x = x_hi * 2 + x_lo), y: 4, z: 4, core: 2. Of those that a mesh axis runs over, the one named last changes fastest.
Arguments:
- objective_grad: float32 [256, 64, 6, 256], P('circ', 'radax'), may hold values from -6 to 6
- adjoint_start: float32 [256, 64, 6, 256], P('circ', 'radax'), may hold values from -6 to 6
- jac_off: bfloat16 [6, 6, 256, 64, 6, 256], P(None, None, 'circ', 'radax'), may hold values from -0.625 to 0.625
- jac_diag: bfloat16 [6, 256, 64, 6, 256], P(None, 'circ', 'radax'), may hold values from -3 to 3, as said below
- precond: bfloat16 [6, 256, 64, 6, 256], P(None, 'circ', 'radax'), may hold values from -1 to 1
- face_cell: int32 [65536], P(('circ', 'radax')), may hold values from 0 to 32767
- face_side: int32 [65536], P(('circ', 'radax')), may hold values from 0 to 1
- design_grad: float32 [65536, 6, 128], P(('circ', 'radax')), may hold values from -0.0546875 to 0.0546875
Outputs:
- adjoint: float32 [256, 64, 6, 256], P('circ', 'radax')
- sensitivity: float32 [32, 128], P('circ', 'radax')
The draws below stay inside these ranges and needn't reach their ends.
Inputs may be any that keep to these rules, and one draw needn't show every extreme that they name: face_cell indexes the cells of the device that holds the face. `jac_diag`: diagonal blocks: each diagonal entry between 1.5 and 3, off-diagonal entries of moderate size.
All inputs are finite; a program needn't handle non-finite values.
Results may differ from the reference program's by a relative error of at most 0.0003.
Values sent between devices are 32-bit elements; how exact they have to be, the bound alone decides.
No kernel may reach another device: no remote copies, remote signals or barrier semaphores. Data moves between devices by JAX's collectives and lax.ppermute only.
A program may use at most 256 MiB of HBM per device.

```python
import jax
import jax.numpy as jnp
from jax import lax

NV = 6
NDV = 128
CTH = 8
CRAD = 16
CAX = 256
FACE_DEV = 512
ITERS = 2
NTH = 256
NRAD = 64
NAX = 256
FACES = 65536
BLADES = 32
N_RADAX = 4


def dominant_blocks(key, low, high, spread):
    shape = (NV, NTH, NRAD, NV, NAX)
    first_key = jax.random.fold_in(key, 11)
    second_key = jax.random.fold_in(key, 23)
    identity = jnp.eye(NV, dtype=jnp.float32)[:, None, None, :, None]
    diagonal = jax.random.uniform(first_key, shape, jnp.float32, low, high)
    others = jnp.clip(jax.random.normal(second_key, shape, jnp.float32), -4.0, 4.0) * spread
    return identity * diagonal + (1.0 - identity) * others


def draw_jac_diag(key, part):
    return dominant_blocks(key, 1.5, 3.0, 0.4).astype(jnp.bfloat16)


def draw_precond(key, part):
    return dominant_blocks(key, 0.3, 0.6, 0.06).astype(jnp.bfloat16)


def set_ends(values, key, smallest, high):
    place = [jax.random.randint(jax.random.fold_in(key, axis), (), 0, length) for axis, length in enumerate(values.shape)]
    longest = values.shape.index(max(values.shape))
    neighbour = place[:longest] + [(place[longest] + 1) % values.shape[longest]] + place[longest + 1:]
    return values.at[tuple(place)].set(smallest).at[tuple(neighbour)].set(high)


def block_scale(key, dims, split, low, largest):
    factor_of = 1.0
    for position, blocks in split:
        draws = jax.random.uniform(jax.random.fold_in(jax.random.fold_in(key, 6), position), (blocks,), jnp.float32, low / len(split), largest / len(split))
        factor_of = factor_of * jnp.repeat(jnp.exp(draws), dims[position] // blocks).reshape((-1,) + (1,) * (len(dims) - 1 - position))
    return factor_of


def bell_draw(rng, shape, scale, reach, split=(), kind=jnp.bfloat16):
    gain = block_scale(rng, shape, split, -0.22, 0.18) if split else 1.0
    array = jax.random.normal(rng, shape, jnp.float32) * scale * gain
    return jnp.minimum(jnp.maximum(array, -reach), reach).astype(kind)


def setup_inputs(seed: int = 0) -> dict:
    splits = jax.random.split(jax.random.key(seed), 9)
    return {
        "objective_grad": bell_draw(splits[0], (NTH, NRAD, NV, NAX), 1.0, 6.0, ((0, 32), (1, 4)), jnp.float32),
        "adjoint_start": bell_draw(splits[1], (NTH, NRAD, NV, NAX), 1.0, 6.0, ((0, 32), (1, 4)), jnp.float32),
        "jac_off": bell_draw(splits[2], (6, NV, NTH, NRAD, NV, NAX), 100 ** -0.5, 0.625, ((2, 32), (3, 4))),
        "jac_diag": draw_jac_diag(jax.random.fold_in(splits[8], 71), 0),
        "precond": draw_precond(jax.random.fold_in(splits[8], 71), 0),
        "face_cell": set_ends(jax.random.randint(splits[5], (FACES,), 0, CTH * CRAD * CAX), jax.random.fold_in(splits[5], 1), 0, (CTH * CRAD * CAX) - 1).astype(jnp.int32),
        "face_side": set_ends(jax.random.randint(splits[6], (FACES,), 0, 2), jax.random.fold_in(splits[6], 1), 0, 1).astype(jnp.int32),
        "design_grad": bell_draw(splits[7], (FACES, NV, NDV), (NV * FACE_DEV * N_RADAX) ** -0.5, 0.0546875, ((0, 128),), jnp.float32),
    }


def block_apply(blocks, vector):
    summed = blocks[0].astype(jnp.float32) * vector[:, :, 0:1, :]
    for column in range(1, NV):
        summed = summed + blocks[column].astype(jnp.float32) * vector[:, :, column:column + 1, :]
    return summed


def neighbour_fields(field):
    zeros_rad = jnp.zeros_like(field[:, :1])
    zeros_ax = jnp.zeros_like(field[..., :1])
    circ_lower = jnp.roll(field, 1, axis=0)
    circ_upper = jnp.roll(field, -1, axis=0)
    rad_lower = jnp.concatenate([zeros_rad, field[:, :-1]], axis=1)
    rad_upper = jnp.concatenate([field[:, 1:], zeros_rad], axis=1)
    ax_lower = jnp.concatenate([zeros_ax, field[..., :-1]], axis=3)
    ax_upper = jnp.concatenate([field[..., 1:], zeros_ax], axis=3)
    return [circ_lower, circ_upper, rad_lower, rad_upper, ax_lower, ax_upper]


def reference(objective_grad, adjoint_start, jac_off, jac_diag, precond, face_cell, face_side, design_grad):
    adjoint = adjoint_start
    for iteration in range(ITERS):
        beside = neighbour_fields(adjoint)
        applied = block_apply(jac_diag, adjoint)
        for direction in range(6):
            applied = applied + block_apply(jac_off[direction], beside[direction])
        residual = objective_grad - applied
        adjoint = adjoint + block_apply(precond, residual)
    face_index = jnp.arange(FACES, dtype=jnp.int32)
    device = face_index // FACE_DEV
    circ_of = device // N_RADAX
    radax_of = device % N_RADAX
    local = face_cell.astype(jnp.int32)
    theta = local // (CRAD * CAX)
    radial = (local // CAX) % CRAD
    axial = local % CAX
    picked = adjoint[circ_of * CTH + theta, radax_of * CRAD + radial, :, axial]
    contrib = jnp.einsum("fi,fid->fd", picked, design_grad, precision=lax.Precision.HIGHEST)
    blade = (circ_of + face_side.astype(jnp.int32)) % BLADES
    sensitivity = jax.ops.segment_sum(contrib, blade, num_segments=BLADES)
    return adjoint, sensitivity
```

```python
import functools

import jax
import jax.numpy as jnp
from jax import lax
from jax.experimental import pallas as pl
from jax.experimental.pallas import tpu as pltpu
from jax.sharding import PartitionSpec as P

F32 = jnp.float32
HIGH = lax.Precision.HIGHEST


def _vmem():
    return pl.BlockSpec(memory_space=pltpu.VMEM)


def _smem():
    return pl.BlockSpec(memory_space=pltpu.SMEM)


def _whole(shape):
    return pl.BlockSpec(shape, lambda t: (0,) * len(shape))


def send_faces(adj, even_ref, odd_ref, near_ref, far_ref):
    nt, nv, nq, _ = adj.shape
    c = lax.axis_index("circ")
    r = lax.axis_index("radax")
    t_even = jnp.where(c % 2 == 0, nt - 1, 0)
    even_ref[...] = adj[t_even]
    odd_ref[...] = adj[nt - 1 - t_even]
    up = r % 2 == 0
    for t in range(nt):
        for i in range(nv):
            low = adj[t, i, 0:1, :]
            high = adj[t, i, nq - 1 : nq, :]
            near_ref[i, t : t + 1, :] = jnp.where(up, high, low)
            far_ref[i, t : t + 1, :] = jnp.where(up, low, high)


def faces_kernel(adj_ref, even_ref, odd_ref, near_ref, far_ref):
    send_faces(adj_ref, even_ref, odd_ref, near_ref, far_ref)


def shift_lanes(plane, step):
    width = plane.shape[1]
    lane = lax.broadcasted_iota(jnp.int32, plane.shape, 1)
    edge = 0 if step == 1 else width - 1
    return jnp.where(lane == edge, 0.0, pltpu.roll(plane, step % width, 1))


def shift_rows(plane, step):
    rows = plane.shape[0]
    row = lax.broadcasted_iota(jnp.int32, plane.shape, 0)
    edge = 0 if step == 1 else rows - 1
    return jnp.where(row == edge, 0.0, pltpu.roll(plane, step % rows, 0))


def local_kernel(keep_edges, adj_ref, g_ref, off_ref, diag_ref, pre_ref, out_ref, *edge_refs):
    t = pl.program_id(0)
    nt, nv, nq, _ = adj_ref.shape
    below = jnp.maximum(t - 1, 0)
    above = jnp.minimum(t + 1, nt - 1)
    has_below = (t > 0).astype(F32)
    has_above = (t < nt - 1).astype(F32)
    acc = [g_ref[0, i] for i in range(nv)]
    for j in range(nv):
        here = adj_ref[t, j]
        fields = [
            adj_ref[below, j] * has_below,
            adj_ref[above, j] * has_above,
            shift_rows(here, 1),
            shift_rows(here, -1),
            shift_lanes(here, 1),
            shift_lanes(here, -1),
        ]
        for i in range(nv):
            acc[i] = acc[i] - diag_ref[j, 0, i].astype(F32) * here
        for k in range(6):
            for i in range(nv):
                block = off_ref[k, j, 0, i].astype(F32)
                acc[i] = acc[i] - block * fields[k]
                if keep_edges and k == 2:
                    edge_refs[0][j, i, pl.ds(t, 1), :] = block[0:1, :]
                if keep_edges and k == 3:
                    edge_refs[1][j, i, pl.ds(t, 1), :] = block[nq - 1 : nq, :]
    new = [adj_ref[t, i] for i in range(nv)]
    for j in range(nv):
        for i in range(nv):
            block = pre_ref[j, 0, i].astype(F32)
            new[i] = new[i] + block * acc[j]
            if keep_edges:
                edge_refs[2][j, i, pl.ds(t, 1), :] = block[0:1, :]
                edge_refs[3][j, i, pl.ds(t, 1), :] = block[nq - 1 : nq, :]
    for i in range(nv):
        out_ref[0, i] = new[i]


def local_part(adj, g, off, diag, pre, keep_edges):
    nt, nv, nq, na = adj.shape
    layer = pl.BlockSpec((1, nv, nq, na), lambda t: (t, 0, 0, 0))
    blocks = pl.BlockSpec((nv, 1, nv, nq, na), lambda t: (0, t, 0, 0, 0))
    out_shape = [jax.ShapeDtypeStruct(adj.shape, F32)]
    out_specs = [layer]
    if keep_edges:
        edge = (nv, nv, nt, na)
        out_shape += [jax.ShapeDtypeStruct(edge, F32)] * 4
        out_specs += [_whole(edge)] * 4
    return pl.pallas_call(
        functools.partial(local_kernel, keep_edges),
        grid=(nt,),
        in_specs=[
            _whole(adj.shape),
            layer,
            pl.BlockSpec((6, nv, 1, nv, nq, na), lambda t: (0, 0, t, 0, 0, 0)),
            blocks,
            blocks,
        ],
        out_specs=out_specs,
        out_shape=out_shape,
        compiler_params=pltpu.CompilerParams(vmem_limit_bytes=24 << 20),
        cost_estimate=pl.CostEstimate(flops=40_000_000, bytes_accessed=24_000_000, transcendentals=0),
        name="local_first" if keep_edges else "local_second",
    )(adj, g, off, diag, pre)


def apply_blocks(load, vectors):
    nv = len(vectors)
    out = []
    for i in range(nv):
        total = load(0, i) * vectors[0]
        for j in range(1, nv):
            total = total + load(j, i) * vectors[j]
        out.append(total)
    return out


def add_halos(adj_ref, even, odd, near, far, off_low, off_up, pre_first, pre_last, edges, out_ref):
    nt, nv, nq, _ = adj_ref.shape
    c = lax.axis_index("circ")
    r = lax.axis_index("radax")
    c_even = c % 2 == 0
    r_even = r % 2 == 0
    out_ref[...] = adj_ref[...]
    for t, low in ((0, True), (nt - 1, False)):
        off, pre = (off_low, pre_first) if low else (off_up, pre_last)
        pick = jnp.logical_not(c_even) if low else c_even
        halo = [jnp.where(pick, even[j], odd[j]) for j in range(nv)]
        extra = apply_blocks(lambda j, i: off[0, j, 0, i].astype(F32), halo)
        change = apply_blocks(lambda j, i: pre[j, 0, i].astype(F32), extra)
        for i in range(nv):
            out_ref[t, i] = out_ref[t, i] - change[i]
    last = lax.axis_size("radax") - 1
    for q, low in ((0, True), (nq - 1, False)):
        off, pre = (edges[0], edges[2]) if low else (edges[1], edges[3])
        pick = jnp.logical_not(r_even) if low else r_even
        inside = (r > 0) if low else (r < last)
        halo = [jnp.where(inside, jnp.where(pick, near[j], far[j]), 0.0) for j in range(nv)]
        extra = apply_blocks(lambda j, i: off[j, i], halo)
        change = apply_blocks(lambda j, i: pre[j, i], extra)
        for t in range(nt):
            for i in range(nv):
                out_ref[t, i, q : q + 1, :] = out_ref[t, i, q : q + 1, :] - change[i][t : t + 1, :]


def halo_kernel(adj_ref, even, odd, near, far, off_low, off_up, pre_first, pre_last, e0, e1, e2, e3,
                out_ref, even_out, odd_out, near_out, far_out):
    add_halos(adj_ref, even, odd, near, far, off_low, off_up, pre_first, pre_last, (e0, e1, e2, e3), out_ref)
    send_faces(out_ref, even_out, odd_out, near_out, far_out)


def final_kernel(adj_ref, even, odd, near, far, off_low, off_up, pre_first, pre_last, e0, e1, e2, e3,
                 cell_ref, side_ref, design_ref, out_ref, lower_ref, upper_ref, by_cell, picked):
    add_halos(adj_ref, even, odd, near, far, off_low, off_up, pre_first, pre_last, (e0, e1, e2, e3), out_ref)
    nt, nv, nq, na = adj_ref.shape
    halves = na // 128
    for t in range(nt):
        for i in range(nv):
            for qt in range(nq // 8):
                for h in range(halves):
                    first = ((t * nq + qt * 8) * halves + h) * 8 + i
                    by_cell[pl.ds(first, 8, stride=8 * halves), :] = out_ref[
                        t, i, qt * 8 : qt * 8 + 8, h * 128 : h * 128 + 128
                    ]
    faces = design_ref.shape[1]
    lane = lax.broadcasted_iota(jnp.int32, (8, 128), 1)

    def pick(f, carry):
        cell = cell_ref[f]
        row = pl.multiple_of((cell // 128) * 8, 8)
        tile = by_cell[pl.ds(row, 8), :]
        kept = jnp.where(lane == cell % 128, tile, 0.0)
        picked[pl.ds(f, 8, stride=faces), :] = kept
        return carry

    lax.fori_loop(0, faces, pick, 0, unroll=16)
    total = jnp.zeros((8, 128), F32)
    sides = lax.broadcasted_iota(jnp.int32, (8, 128), 0)
    for f0 in range(0, faces, 128):
        contrib = jnp.zeros((128, 128), F32)
        for i in range(nv):
            value = jnp.sum(picked[i * faces + f0 : i * faces + f0 + 128, :], axis=1, keepdims=True)
            contrib = contrib + value * design_ref[i, f0 : f0 + 128, :]
        table = (side_ref[f0 // 128 : f0 // 128 + 1, :] == sides).astype(F32)
        total = total + jnp.dot(table, contrib, precision=HIGH, preferred_element_type=F32)
    lower_ref[...] = total[0:1, :]
    upper_ref[...] = total[1:2, :]


def halo_part(adj, halos, off, pre, edges, faces=None):
    nt, nv, nq, na = adj.shape
    one = (1, nv, 1, nv, nq, na)
    layer = (nv, 1, nv, nq, na)
    in_specs = [_whole(adj.shape)] + [_whole(h.shape) for h in halos]
    in_specs += [
        pl.BlockSpec(one, lambda s: (0, 0, 0, 0, 0, 0)),
        pl.BlockSpec(one, lambda s: (1, 0, nt - 1, 0, 0, 0)),
        pl.BlockSpec(layer, lambda s: (0, 0, 0, 0, 0)),
        pl.BlockSpec(layer, lambda s: (0, nt - 1, 0, 0, 0)),
    ]
    in_specs += [_whole(e.shape) for e in edges]
    args = [adj, *halos, off, off, pre, pre, *edges]
    params = pltpu.CompilerParams(vmem_limit_bytes=24 << 20)
    cost = pl.CostEstimate(flops=4_000_000, bytes_accessed=5_000_000, transcendentals=0)
    if faces is None:
        out_shape = [jax.ShapeDtypeStruct(adj.shape, F32)]
        out_shape += [jax.ShapeDtypeStruct(h.shape, F32) for h in halos]
        return pl.pallas_call(
            halo_kernel, grid=(1,), in_specs=in_specs,
            out_specs=[_whole(o.shape) for o in out_shape], out_shape=out_shape,
            compiler_params=params, cost_estimate=cost, name="halo_first",
        )(*args)
    cell, side, design = faces
    ndv = design.shape[2]
    out_shape = [jax.ShapeDtypeStruct(adj.shape, F32)] + [jax.ShapeDtypeStruct((1, ndv), F32)] * 2
    return pl.pallas_call(
        final_kernel, grid=(1,),
        in_specs=in_specs + [_smem(), _whole(side.shape), _whole(design.shape)],
        out_specs=[_whole(o.shape) for o in out_shape], out_shape=out_shape,
        scratch_shapes=[
            pltpu.VMEM((nt * nq * na // 128 * 8, 128), F32),
            pltpu.VMEM((8 * design.shape[1], 128), F32),
        ],
        compiler_params=params, cost_estimate=cost, name="halo_last",
    )(*args, cell, side, design)


def swap_halos(even, odd, near, far):
    nc = lax.axis_size("circ")
    nr = lax.axis_size("radax")
    odd = lax.ppermute(odd, "circ", [(i, (i + 1) % nc if i % 2 else (i - 1) % nc) for i in range(nc)])
    far = lax.ppermute(far, "radax", [(i, nr - 1 - i) for i in range(nr)])
    even = lax.ppermute(even, "circ", [(i, i ^ 1) for i in range(nc)])
    near = lax.ppermute(near, "radax", [(i, i ^ 1) for i in range(nr)])
    return even, odd, near, far


def body(objective_grad, adjoint_start, jac_off, jac_diag, precond, face_cell, face_side, design_grad):
    g = objective_grad.transpose(0, 2, 1, 3)
    adj = adjoint_start.transpose(0, 2, 1, 3)
    off = jac_off.transpose(0, 1, 2, 4, 3, 5)
    diag = jac_diag.transpose(0, 1, 3, 2, 4)
    pre = precond.transpose(0, 1, 3, 2, 4)
    design = design_grad.transpose(1, 0, 2)
    nt, nv, nq, na = adj.shape
    ring = jax.ShapeDtypeStruct((nv, nq, na), F32)
    rows = jax.ShapeDtypeStruct((nv, nt, na), F32)
    sends = pl.pallas_call(
        faces_kernel, in_specs=[_vmem()], out_specs=[_vmem()] * 4,
        out_shape=[ring, ring, rows, rows], name="faces",
    )(adj)
    halos = swap_halos(*sends)
    part, *edges = local_part(adj, g, off, diag, pre, True)
    adj, *sends = halo_part(part, halos, off, pre, edges)
    halos = swap_halos(*sends)
    (part,) = local_part(adj, g, off, diag, pre, False)
    side = face_side.reshape(-1, 128)
    adj, lower, upper = halo_part(part, halos, off, pre, edges, (face_cell, side, design))
    nc = lax.axis_size("circ")
    nr = lax.axis_size("radax")
    total = lower + lax.ppermute(upper, "circ", [(i, (i + 1) % nc) for i in range(nc)])
    total = total + lax.ppermute(total, "radax", [(i, i ^ 1) for i in range(nr)])
    total = total + lax.ppermute(total, "radax", [(i, i ^ 2) for i in range(nr)])
    owned = total.shape[1] // nr
    sensitivity = lax.dynamic_slice_in_dim(total, lax.axis_index("radax") * owned, owned, 1)
    return adj.transpose(0, 2, 1, 3), sensitivity


def solution(mesh):
    in_specs = (
        P("circ", "radax", None, None),
        P("circ", "radax", None, None),
        P(None, None, "circ", "radax", None, None),
        P(None, "circ", "radax", None, None),
        P(None, "circ", "radax", None, None),
        P(("circ", "radax")),
        P(("circ", "radax")),
        P(("circ", "radax"), None, None),
    )
    out_specs = (P("circ", "radax", None, None), P("circ", "radax"))
    return jax.shard_map(body, mesh=mesh, in_specs=in_specs, out_specs=out_specs, check_vma=False)
```

```python
import functools

import jax
import jax.numpy as jnp
from jax import lax
from jax.experimental import pallas as pl
from jax.experimental.pallas import tpu as pltpu
from jax.sharding import PartitionSpec as P

F32 = jnp.float32
PARAMS = pltpu.CompilerParams(vmem_limit_bytes=28 << 20)


def _vmem():
    return pl.BlockSpec(memory_space=pltpu.VMEM)


def _smem():
    return pl.BlockSpec(memory_space=pltpu.SMEM)


def send_faces(adj, even_ref, odd_ref, near_ref, far_ref):
    nt, nv, nq, _ = adj.shape
    c = lax.axis_index("circ")
    r = lax.axis_index("radax")
    t_even = jnp.where(c % 2 == 0, nt - 1, 0)
    even_ref[...] = adj[t_even]
    odd_ref[...] = adj[nt - 1 - t_even]
    up = r % 2 == 0
    for t in range(nt):
        for i in range(nv):
            low = adj[t, i, 0:1, :]
            high = adj[t, i, nq - 1 : nq, :]
            near_ref[i, t : t + 1, :] = jnp.where(up, high, low)
            far_ref[i, t : t + 1, :] = jnp.where(up, low, high)


def faces_kernel(adj_ref, even_ref, odd_ref, near_ref, far_ref):
    send_faces(adj_ref, even_ref, odd_ref, near_ref, far_ref)


def shift_lanes(plane, step):
    width = plane.shape[1]
    lane = lax.broadcasted_iota(jnp.int32, plane.shape, 1)
    edge = 0 if step == 1 else width - 1
    return jnp.where(lane == edge, 0.0, pltpu.roll(plane, step % width, 1))


def shift_rows(plane, step):
    rows = plane.shape[0]
    row = lax.broadcasted_iota(jnp.int32, plane.shape, 0)
    edge = 0 if step == 1 else rows - 1
    return jnp.where(row == edge, 0.0, pltpu.roll(plane, step % rows, 0))


def local_layer(t, adj_ref, g_ref, off_ref, diag_ref, pre_ref, out_ref, edge_refs=()):
    nt, nv, nq, _ = adj_ref.shape
    below = jnp.maximum(t - 1, 0)
    above = jnp.minimum(t + 1, nt - 1)
    has_below = (t > 0).astype(F32)
    has_above = (t < nt - 1).astype(F32)
    acc = [g_ref[t, i] for i in range(nv)]
    for j in range(nv):
        here = adj_ref[t, j]
        fields = [
            adj_ref[below, j] * has_below,
            adj_ref[above, j] * has_above,
            shift_rows(here, 1),
            shift_rows(here, -1),
            shift_lanes(here, 1),
            shift_lanes(here, -1),
        ]
        for i in range(nv):
            acc[i] = acc[i] - diag_ref[j, t, i].astype(F32) * here
        for k in range(6):
            for i in range(nv):
                block = off_ref[k, j, t, i].astype(F32)
                acc[i] = acc[i] - block * fields[k]
                if edge_refs and k == 2:
                    edge_refs[0][j, i, pl.ds(t, 1), :] = block[0:1, :]
                if edge_refs and k == 3:
                    edge_refs[1][j, i, pl.ds(t, 1), :] = block[nq - 1 : nq, :]
    new = [adj_ref[t, i] for i in range(nv)]
    for j in range(nv):
        for i in range(nv):
            block = pre_ref[j, t, i].astype(F32)
            new[i] = new[i] + block * acc[j]
            if edge_refs:
                edge_refs[2][j, i, pl.ds(t, 1), :] = block[0:1, :]
                edge_refs[3][j, i, pl.ds(t, 1), :] = block[nq - 1 : nq, :]
    for i in range(nv):
        out_ref[t, i] = new[i]


def first_kernel(adj_hbm, g_hbm, off_hbm, diag_hbm, pre_hbm,
                 out_ref, e0, e1, e2, e3, g_ref, off_ref, diag_ref, pre_ref, adj_ref, sems):
    nt = adj_ref.shape[0]

    def copies(t):
        return [
            pltpu.make_async_copy(off_hbm.at[:, :, t], off_ref.at[:, :, t], sems.at[0, t]),
            pltpu.make_async_copy(diag_hbm.at[:, t], diag_ref.at[:, t], sems.at[1, t]),
            pltpu.make_async_copy(pre_hbm.at[:, t], pre_ref.at[:, t], sems.at[2, t]),
            pltpu.make_async_copy(g_hbm.at[t], g_ref.at[t], sems.at[3, t]),
        ]

    whole = pltpu.make_async_copy(adj_hbm, adj_ref, sems.at[4, 0])
    whole.start()
    for t in range(nt):
        for copy in copies(t):
            copy.start()
    whole.wait()

    def layer(t, carry):
        for copy in copies(t):
            copy.wait()
        local_layer(t, adj_ref, g_ref, off_ref, diag_ref, pre_ref, out_ref, (e0, e1, e2, e3))
        return carry

    lax.fori_loop(0, nt, layer, 0)


def second_kernel(adj_ref, g_ref, off_ref, diag_ref, pre_ref, out_ref):
    def layer(t, carry):
        local_layer(t, adj_ref, g_ref, off_ref, diag_ref, pre_ref, out_ref)
        return carry

    lax.fori_loop(0, adj_ref.shape[0], layer, 0)


COST = pl.CostEstimate(flops=40_000_000, bytes_accessed=24_000_000, transcendentals=0)


def first_part(adj, g, off, diag, pre):
    nt, nv, nq, na = adj.shape
    out_shape = [jax.ShapeDtypeStruct(adj.shape, F32)]
    out_shape += [jax.ShapeDtypeStruct((nv, nv, nt, na), F32)] * 4
    out_shape += [pltpu.VMEM(x.shape, x.dtype) for x in (g, off, diag, pre)]
    return pl.pallas_call(
        first_kernel,
        in_specs=[pl.BlockSpec(memory_space=pltpu.HBM)] * 5,
        out_specs=[_vmem()] * len(out_shape),
        out_shape=out_shape,
        scratch_shapes=[pltpu.VMEM(adj.shape, F32), pltpu.SemaphoreType.DMA((5, nt))],
        compiler_params=PARAMS,
        cost_estimate=COST,
        name="local_first",
    )(adj, g, off, diag, pre)


def second_part(adj, g, off, diag, pre):
    return pl.pallas_call(
        second_kernel,
        in_specs=[_vmem()] * 5,
        out_specs=_vmem(),
        out_shape=jax.ShapeDtypeStruct(adj.shape, F32),
        compiler_params=PARAMS,
        cost_estimate=COST,
        name="local_second",
    )(adj, g, off, diag, pre)


def apply_blocks(load, vectors):
    nv = len(vectors)
    out = []
    for i in range(nv):
        total = load(0, i) * vectors[0]
        for j in range(1, nv):
            total = total + load(j, i) * vectors[j]
        out.append(total)
    return out


def add_halos(adj_ref, even, odd, near, far, off_ref, pre_ref, edges, out_ref):
    nt, nv, nq, _ = adj_ref.shape
    c = lax.axis_index("circ")
    r = lax.axis_index("radax")
    c_even = c % 2 == 0
    r_even = r % 2 == 0
    out_ref[...] = adj_ref[...]
    for t, low in ((0, True), (nt - 1, False)):
        k = 0 if low else 1
        pick = jnp.logical_not(c_even) if low else c_even
        halo = [jnp.where(pick, even[j], odd[j]) for j in range(nv)]
        extra = apply_blocks(lambda j, i: off_ref[k, j, t, i].astype(F32), halo)
        change = apply_blocks(lambda j, i: pre_ref[j, t, i].astype(F32), extra)
        for i in range(nv):
            out_ref[t, i] = out_ref[t, i] - change[i]
    last = lax.axis_size("radax") - 1
    for q, low in ((0, True), (nq - 1, False)):
        off, pre = (edges[0], edges[2]) if low else (edges[1], edges[3])
        pick = jnp.logical_not(r_even) if low else r_even
        inside = (r > 0) if low else (r < last)
        halo = [jnp.where(inside, jnp.where(pick, near[j], far[j]), 0.0) for j in range(nv)]
        extra = apply_blocks(lambda j, i: off[j, i], halo)
        change = apply_blocks(lambda j, i: pre[j, i], extra)
        for t in range(nt):
            for i in range(nv):
                out_ref[t, i, q : q + 1, :] = out_ref[t, i, q : q + 1, :] - change[i][t : t + 1, :]


def halo_kernel(adj_ref, even, odd, near, far, off_ref, pre_ref, e0, e1, e2, e3,
                out_ref, even_out, odd_out, near_out, far_out):
    add_halos(adj_ref, even, odd, near, far, off_ref, pre_ref, (e0, e1, e2, e3), out_ref)
    send_faces(out_ref, even_out, odd_out, near_out, far_out)


def final_kernel(adj_ref, even, odd, near, far, off_ref, pre_ref, e0, e1, e2, e3,
                 side_ref, design_ref, cell_ref, out_ref, sums_ref, by_cell, picked):
    add_halos(adj_ref, even, odd, near, far, off_ref, pre_ref, (e0, e1, e2, e3), out_ref)
    nt, nv, nq, na = adj_ref.shape
    halves = na // 128
    for t in range(nt):
        for i in range(nv):
            for qt in range(nq // 8):
                for h in range(halves):
                    first = ((t * nq + qt * 8) * halves + h) * 8 + i
                    by_cell[pl.ds(first, 8, stride=8 * halves), :] = out_ref[
                        t, i, qt * 8 : qt * 8 + 8, h * 128 : h * 128 + 128
                    ]
    faces = design_ref.shape[1]
    lane = lax.broadcasted_iota(jnp.int32, (8, 128), 1)

    def pick(f, carry):
        cell = cell_ref[f]
        row = pl.multiple_of(lax.shift_right_logical(cell, 7) * 8, 8)
        tile = by_cell[pl.ds(row, 8), :]
        kept = jnp.where(lane == (cell & 127), tile, 0.0)
        picked[pl.ds(f, 8, stride=faces), :] = kept
        return carry

    lax.fori_loop(0, faces, pick, 0, unroll=32)
    every = jnp.zeros((8, 128), F32)
    upper = jnp.zeros((8, 128), F32)
    for f0 in range(0, faces, 128):
        on_upper = jnp.transpose(jnp.broadcast_to(side_ref[f0 // 128 : f0 // 128 + 1, :].astype(F32), (128, 128)))
        contrib = jnp.zeros((128, 128), F32)
        for i in range(nv):
            value = jnp.sum(picked[i * faces + f0 : i * faces + f0 + 128, :], axis=1, keepdims=True)
            contrib = contrib + value * design_ref[i, f0 : f0 + 128, :]
        every = every + jnp.sum(contrib.reshape(16, 8, 128), axis=0)
        upper = upper + jnp.sum((contrib * on_upper).reshape(16, 8, 128), axis=0)
    upper = jnp.sum(upper, axis=0, keepdims=True)
    sums_ref[0:1, :] = jnp.sum(every, axis=0, keepdims=True) - upper
    sums_ref[1:2, :] = upper


def halo_part(adj, halos, off, pre, edges, faces=None):
    nt, nv, nq, na = adj.shape
    args = [adj, *halos, off, pre, *edges]
    cost = pl.CostEstimate(flops=4_000_000, bytes_accessed=5_000_000, transcendentals=0)
    out_shape = [jax.ShapeDtypeStruct(adj.shape, F32)]
    if faces is None:
        out_shape += [jax.ShapeDtypeStruct(h.shape, F32) for h in halos]
        return pl.pallas_call(
            halo_kernel, in_specs=[_vmem()] * len(args), out_specs=[_vmem()] * 5, out_shape=out_shape,
            compiler_params=PARAMS, cost_estimate=cost, name="halo_first",
        )(*args)
    cell, side, design = faces
    out_shape += [jax.ShapeDtypeStruct((2, design.shape[2]), F32)]
    return pl.pallas_call(
        final_kernel, in_specs=[_vmem()] * (len(args) + 2) + [_smem()], out_specs=[_vmem()] * 2, out_shape=out_shape,
        scratch_shapes=[
            pltpu.VMEM((nt * nq * na // 128 * 8, 128), F32),
            pltpu.VMEM((8 * design.shape[1], 128), F32),
        ],
        compiler_params=PARAMS, cost_estimate=cost, name="halo_last",
    )(*args, side, design, cell)


def swap_halos(even, odd, near, far):
    nc = lax.axis_size("circ")
    nr = lax.axis_size("radax")
    odd = lax.ppermute(odd, "circ", [(i, (i + 1) % nc if i % 2 else (i - 1) % nc) for i in range(nc)])
    far = lax.ppermute(far, "radax", [(i, nr - 1 - i) for i in range(nr)])
    even = lax.ppermute(even, "circ", [(i, i ^ 1) for i in range(nc)])
    near = lax.ppermute(near, "radax", [(i, i ^ 1) for i in range(nr)])
    return even, odd, near, far


def combine(sums):
    nc = lax.axis_size("circ")
    nr = lax.axis_size("radax")
    near = [(i, i ^ 1) for i in range(nr)]
    both = sums + lax.ppermute(sums, "radax", near)
    lower, upper = both[0:1], both[1:2]
    ring = [(c * nr + r, (c + 1) % nc * nr + (r ^ 2 if r % 2 == 0 else r)) for c in range(nc) for r in range(nr)]
    arrived = lax.ppermute(upper, ("circ", "radax"), ring)
    other = lax.ppermute(lower, "radax", [(i, i ^ 2) for i in range(nr)])
    first = lax.axis_index("radax") % 2 == 0
    mine = arrived + jnp.where(first, lower + other, 0.0)
    return mine + lax.ppermute(mine, "radax", near)


def body(objective_grad, adjoint_start, jac_off, jac_diag, precond, face_cell, face_side, design_grad):
    g = objective_grad.transpose(0, 2, 1, 3)
    adj = adjoint_start.transpose(0, 2, 1, 3)
    off = jac_off.transpose(0, 1, 2, 4, 3, 5)
    diag = jac_diag.transpose(0, 1, 3, 2, 4)
    pre = precond.transpose(0, 1, 3, 2, 4)
    design = design_grad.transpose(1, 0, 2)
    nt, nv, nq, na = adj.shape
    ring = jax.ShapeDtypeStruct((nv, nq, na), F32)
    rows = jax.ShapeDtypeStruct((nv, nt, na), F32)
    sends = pl.pallas_call(
        faces_kernel, in_specs=[_vmem()], out_specs=[_vmem()] * 4,
        out_shape=[ring, ring, rows, rows], name="faces",
        compiler_params=PARAMS,
    )(adj)
    halos = swap_halos(*sends)
    hbm = [pltpu.with_memory_space_constraint(x, pltpu.HBM) for x in (adj, g, off, diag, pre)]
    part, *edges, g, off, diag, pre = first_part(*hbm)
    g, off, diag, pre = [pltpu.with_memory_space_constraint(x, pltpu.VMEM) for x in (g, off, diag, pre)]
    adj, *sends = halo_part(part, halos, off, pre, edges)
    halos = swap_halos(*sends)
    part = second_part(adj, g, off, diag, pre)
    side = face_side.reshape(-1, 128)
    adj, sums = halo_part(part, halos, off, pre, edges, (face_cell, side, design))
    total = combine(sums)
    nr = lax.axis_size("radax")
    owned = total.shape[1] // nr
    sensitivity = lax.dynamic_slice_in_dim(total, lax.axis_index("radax") * owned, owned, 1)
    return adj.transpose(0, 2, 1, 3), sensitivity


def solution(mesh):
    in_specs = (
        P("circ", "radax", None, None),
        P("circ", "radax", None, None),
        P(None, None, "circ", "radax", None, None),
        P(None, "circ", "radax", None, None),
        P(None, "circ", "radax", None, None),
        P(("circ", "radax")),
        P(("circ", "radax")),
        P(("circ", "radax"), None, None),
    )
    out_specs = (P("circ", "radax", None, None), P("circ", "radax"))
    return jax.shard_map(body, mesh=mesh, in_specs=in_specs, out_specs=out_specs, check_vma=False)
```

```python
import jax
import jax.numpy as jnp
from jax import lax
from jax.experimental import pallas as pl
from jax.experimental.pallas import tpu as pltpu
from jax.sharding import PartitionSpec as P


F32 = jnp.float32
PARAMS = pltpu.CompilerParams(vmem_limit_bytes=28 << 20)


def _vmem():
    return pl.BlockSpec(memory_space=pltpu.VMEM)


def send_faces(adj, even_ref, odd_ref, near_ref, far_ref):
    nt, nv, nq, _ = adj.shape
    c = lax.axis_index("circ")
    r = lax.axis_index("radax")
    t_even = jnp.where(c % 2 == 0, nt - 1, 0)
    even_ref[...] = adj[t_even]
    odd_ref[...] = adj[nt - 1 - t_even]
    up = r % 2 == 0
    for t in range(nt):
        for i in range(nv):
            low = adj[t, i, 0:1, :]
            high = adj[t, i, nq - 1 : nq, :]
            near_ref[i, t : t + 1, :] = jnp.where(up, high, low)
            far_ref[i, t : t + 1, :] = jnp.where(up, low, high)


def faces_kernel(adj_hbm, adj_ref, even_ref, odd_ref, near_ref, far_ref, sem):
    copy = pltpu.make_async_copy(adj_hbm, adj_ref, sem)
    copy.start()
    copy.wait()
    send_faces(adj_ref, even_ref, odd_ref, near_ref, far_ref)


def shift_lanes(plane, step):
    width = plane.shape[1]
    lane = lax.broadcasted_iota(jnp.int32, plane.shape, 1)
    edge = 0 if step == 1 else width - 1
    return jnp.where(lane == edge, 0.0, pltpu.roll(plane, step % width, 1))


def shift_rows(plane, step):
    rows = plane.shape[0]
    row = lax.broadcasted_iota(jnp.int32, plane.shape, 0)
    edge = 0 if step == 1 else rows - 1
    return jnp.where(row == edge, 0.0, pltpu.roll(plane, step % rows, 0))


def local_layer(t, adj_ref, g_ref, off_ref, diag_ref, pre_ref, out_ref, edge_refs=(), wait=None):
    nt, nv, nq, _ = adj_ref.shape
    below = jnp.maximum(t - 1, 0)
    above = jnp.minimum(t + 1, nt - 1)
    has_below = (t > 0).astype(F32)
    has_above = (t < nt - 1).astype(F32)
    acc = [jnp.zeros(adj_ref.shape[2:], F32)] * nv
    for j in range(nv):
        here = adj_ref[t, j]
        fields = [
            adj_ref[below, j] * has_below,
            adj_ref[above, j] * has_above,
            shift_rows(here, 1),
            shift_rows(here, -1),
            shift_lanes(here, 1),
            shift_lanes(here, -1),
        ]
        for k in range(6):
            for i in range(nv):
                block = off_ref[k, j, t, i].astype(F32)
                acc[i] = acc[i] + block * fields[k]
                if edge_refs and k == 2:
                    edge_refs[0][j, i, pl.ds(t, 1), :] = block[0:1, :]
                if edge_refs and k == 3:
                    edge_refs[1][j, i, pl.ds(t, 1), :] = block[nq - 1 : nq, :]
    if wait is not None:
        wait()
    for j in range(nv):
        here = adj_ref[t, j]
        for i in range(nv):
            acc[i] = acc[i] + diag_ref[j, t, i].astype(F32) * here
    acc = [g_ref[t, i] - acc[i] for i in range(nv)]
    new = [adj_ref[t, i] for i in range(nv)]
    for j in range(nv):
        for i in range(nv):
            block = pre_ref[j, t, i].astype(F32)
            new[i] = new[i] + block * acc[j]
            if edge_refs:
                edge_refs[2][j, i, pl.ds(t, 1), :] = block[0:1, :]
                edge_refs[3][j, i, pl.ds(t, 1), :] = block[nq - 1 : nq, :]
    for i in range(nv):
        out_ref[t, i] = new[i]


def first_kernel(adj_ref, off_ref, g_hbm, diag_hbm, pre_hbm,
                 out_ref, e0, e1, e2, e3, g_ref, diag_ref, pre_ref, sems):
    nt = adj_ref.shape[0]

    def copies(t):
        return [
            pltpu.make_async_copy(g_hbm.at[t], g_ref.at[t], sems.at[0, t]),
            pltpu.make_async_copy(diag_hbm.at[:, t], diag_ref.at[:, t], sems.at[1, t]),
            pltpu.make_async_copy(pre_hbm.at[:, t], pre_ref.at[:, t], sems.at[2, t]),
        ]

    for t in range(nt):
        for copy in copies(t):
            copy.start()

    def layer(t, carry):
        def wait():
            for copy in copies(t):
                copy.wait()

        local_layer(t, adj_ref, g_ref, off_ref, diag_ref, pre_ref, out_ref, (e0, e1, e2, e3), wait)
        return carry

    lax.fori_loop(0, nt, layer, 0)


def second_kernel(adj_ref, g_ref, off_ref, diag_ref, pre_ref, out_ref):
    def layer(t, carry):
        local_layer(t, adj_ref, g_ref, off_ref, diag_ref, pre_ref, out_ref)
        return carry

    lax.fori_loop(0, adj_ref.shape[0], layer, 0)


COST = pl.CostEstimate(flops=40_000_000, bytes_accessed=24_000_000, transcendentals=0)


def first_part(adj, off, g, diag, pre):
    nt, nv, _, na = adj.shape
    out_shape = [jax.ShapeDtypeStruct(adj.shape, F32)]
    out_shape += [jax.ShapeDtypeStruct((nv, nv, nt, na), F32)] * 4
    out_shape += [pltpu.VMEM(x.shape, x.dtype) for x in (g, diag, pre)]
    return pl.pallas_call(
        first_kernel,
        in_specs=[_vmem()] * 2 + [pl.BlockSpec(memory_space=pltpu.HBM)] * 3,
        out_specs=[_vmem()] * len(out_shape),
        out_shape=out_shape,
        scratch_shapes=[pltpu.SemaphoreType.DMA((3, nt))],
        compiler_params=PARAMS,
        cost_estimate=COST,
        name="local_first",
    )(adj, off, g, diag, pre)


def second_part(adj, g, off, diag, pre):
    return pl.pallas_call(
        second_kernel,
        in_specs=[_vmem()] * 5,
        out_specs=_vmem(),
        out_shape=jax.ShapeDtypeStruct(adj.shape, F32),
        compiler_params=PARAMS,
        cost_estimate=COST,
        name="local_second",
    )(adj, g, off, diag, pre)


def apply_blocks(load, vectors):
    nv = len(vectors)
    out = []
    for i in range(nv):
        total = load(0, i) * vectors[0]
        for j in range(1, nv):
            total = total + load(j, i) * vectors[j]
        out.append(total)
    return out


def add_halos(adj_ref, even, odd, near, far, off_ref, pre_ref, edges, out_ref):
    nt, nv, nq, _ = adj_ref.shape
    c = lax.axis_index("circ")
    r = lax.axis_index("radax")
    c_even = c % 2 == 0
    r_even = r % 2 == 0
    out_ref[...] = adj_ref[...]
    for t, low in ((0, True), (nt - 1, False)):
        k = 0 if low else 1
        pick = jnp.logical_not(c_even) if low else c_even
        halo = [jnp.where(pick, even[j], odd[j]) for j in range(nv)]
        extra = apply_blocks(lambda j, i: off_ref[k, j, t, i].astype(F32), halo)
        change = apply_blocks(lambda j, i: pre_ref[j, t, i].astype(F32), extra)
        for i in range(nv):
            out_ref[t, i] = out_ref[t, i] - change[i]
    last = lax.axis_size("radax") - 1
    for q, low in ((0, True), (nq - 1, False)):
        off, pre = (edges[0], edges[2]) if low else (edges[1], edges[3])
        pick = jnp.logical_not(r_even) if low else r_even
        inside = (r > 0) if low else (r < last)
        halo = [jnp.where(inside, jnp.where(pick, near[j], far[j]), 0.0) for j in range(nv)]
        extra = apply_blocks(lambda j, i: off[j, i], halo)
        change = apply_blocks(lambda j, i: pre[j, i], extra)
        for t in range(nt):
            for i in range(nv):
                out_ref[t, i, q : q + 1, :] = out_ref[t, i, q : q + 1, :] - change[i][t : t + 1, :]


def halo_kernel(adj_ref, even, odd, near, far, off_ref, pre_ref, e0, e1, e2, e3,
                out_ref, even_out, odd_out, near_out, far_out):
    add_halos(adj_ref, even, odd, near, far, off_ref, pre_ref, (e0, e1, e2, e3), out_ref)
    send_faces(out_ref, even_out, odd_out, near_out, far_out)


def final_kernel(adj_ref, even, odd, near, far, off_ref, pre_ref, e0, e1, e2, e3,
                 side_ref, design_ref, cell_ref, out_hbm, sums_ref, out_ref, by_cell, places, table, sems):
    nt, nv, nq, na = adj_ref.shape
    chunks = cell_ref.shape[0]
    cell = cell_ref[...]
    lane = lax.broadcasted_iota(jnp.int32, cell.shape, 1)
    places[0:chunks, :] = (cell >> 7) * 8 + (cell >> (na.bit_length() - 1))
    places[chunks : 2 * chunks, :] = (lane - cell) & 127
    look_up = pltpu.make_async_copy(places, table, sems.at[0])
    look_up.start()
    add_halos(adj_ref, even, odd, near, far, off_ref, pre_ref, (e0, e1, e2, e3), out_ref)
    result = pltpu.make_async_copy(out_ref, out_hbm, sems.at[1])
    result.start()
    halves = na // 128
    pitch = 8 * halves + 1
    for t in range(nt):
        for i in range(nv):
            for qt in range(nq // 8):
                for h in range(halves):
                    first = (t * nq + qt * 8) * pitch + h * 8 + i
                    by_cell[pl.ds(first, 8, stride=pitch), :] = out_ref[
                        t, i, qt * 8 : qt * 8 + 8, h * 128 : h * 128 + 128
                    ]
    lane = lax.broadcasted_iota(jnp.int32, (8, 128), 1)
    field = lax.broadcasted_iota(jnp.int32, (8, 128), 0)
    look_up.wait()

    def chunk(k, carry):
        every, upper = carry
        side = jnp.broadcast_to(side_ref[pl.ds(k, 1), :].astype(F32), (8, 128))
        picked = jnp.zeros((8, 128), F32)
        for f in range(128):
            tile = by_cell[pl.ds(table[k, f], 8), :]
            picked = jnp.where(lane == f, pltpu.roll(tile, table[k + chunks, f], 1), picked)
        by_face = jnp.transpose(jnp.where(field == 6, side, picked))
        contrib = jnp.zeros((128, 128), F32)
        for i in range(nv):
            contrib = contrib + by_face[:, i : i + 1] * design_ref[i, pl.ds(pl.multiple_of(k * 128, 128), 128), :]
        every = every + jnp.sum(contrib.reshape(16, 8, 128), axis=0)
        upper = upper + jnp.sum((contrib * by_face[:, 6:7]).reshape(16, 8, 128), axis=0)
        return every, upper

    zero = jnp.zeros((8, 128), F32)
    every, upper = lax.fori_loop(0, chunks, chunk, (zero, zero))
    upper = jnp.sum(upper, axis=0, keepdims=True)
    sums_ref[0:1, :] = jnp.sum(every, axis=0, keepdims=True) - upper
    sums_ref[1:2, :] = upper
    result.wait()


def halo_part(adj, halos, off, pre, edges, faces=None):
    nt, _, nq, na = adj.shape
    args = [adj, *halos, off, pre, *edges]
    cost = pl.CostEstimate(flops=4_000_000, bytes_accessed=5_000_000, transcendentals=0)
    out_shape = [jax.ShapeDtypeStruct(adj.shape, F32)]
    if faces is None:
        out_shape += [jax.ShapeDtypeStruct(h.shape, F32) for h in halos]
        return pl.pallas_call(
            halo_kernel, in_specs=[_vmem()] * len(args), out_specs=[_vmem()] * 5, out_shape=out_shape,
            compiler_params=PARAMS, cost_estimate=cost, name="halo_first",
        )(*args)
    cell, side, design = faces
    out_shape += [jax.ShapeDtypeStruct((2, design.shape[2]), F32)]
    return pl.pallas_call(
        final_kernel, in_specs=[_vmem()] * (len(args) + 3),
        out_specs=[pl.BlockSpec(memory_space=pltpu.HBM), _vmem()], out_shape=out_shape,
        scratch_shapes=[
            pltpu.VMEM(adj.shape, F32),
            pltpu.VMEM((nt * nq * (na // 16 + 1), 128), F32),
            pltpu.VMEM((2 * cell.shape[0], 128), jnp.int32),
            pltpu.SMEM((2 * cell.shape[0], 128), jnp.int32),
            pltpu.SemaphoreType.DMA((2,)),
        ],
        compiler_params=PARAMS, cost_estimate=cost, name="halo_last",
    )(*args, side, design, cell)


def swap_halos(even, odd, near, far):
    nc = lax.axis_size("circ")
    nr = lax.axis_size("radax")
    odd = lax.ppermute(odd, "circ", [(i, (i + 1) % nc if i % 2 else (i - 1) % nc) for i in range(nc)])
    far = lax.ppermute(far, "radax", [(i, nr - 1 - i) for i in range(nr)])
    even = lax.ppermute(even, "circ", [(i, i ^ 1) for i in range(nc)])
    near = lax.ppermute(near, "radax", [(i, i ^ 1) for i in range(nr)])
    return even, odd, near, far


def combine(sums):
    nc = lax.axis_size("circ")
    nr = lax.axis_size("radax")
    lower, upper = sums[0:1], sums[1:2]

    def ring(flip):
        return [(c * nr + r, (c + 1) % nc * nr + (r ^ flip)) for c in range(nc) for r in range(nr)]

    crossed = lax.ppermute(upper, ("circ", "radax"), ring(2))
    straight = lax.ppermute(upper, ("circ", "radax"), ring(0))
    other = lax.ppermute(lower, "radax", [(i, i ^ 2) for i in range(nr)])
    mine = (lower + other) + (straight + crossed)
    return mine + lax.ppermute(mine, "radax", [(i, i ^ 1) for i in range(nr)])


def body(objective_grad, adjoint_start, jac_off, jac_diag, precond, face_cell, face_side, design_grad):
    g = objective_grad.transpose(0, 2, 1, 3)
    adj = adjoint_start.transpose(0, 2, 1, 3)
    off = jac_off.transpose(0, 1, 2, 4, 3, 5)
    diag = jac_diag.transpose(0, 1, 3, 2, 4)
    pre = precond.transpose(0, 1, 3, 2, 4)
    design = design_grad.transpose(1, 0, 2)
    nt, nv, nq, na = adj.shape
    ring = jax.ShapeDtypeStruct((nv, nq, na), F32)
    rows = jax.ShapeDtypeStruct((nv, nt, na), F32)
    adj, *sends = pl.pallas_call(
        faces_kernel, in_specs=[pl.BlockSpec(memory_space=pltpu.HBM)], out_specs=[_vmem()] * 5,
        out_shape=[pltpu.VMEM(adj.shape, F32), ring, ring, rows, rows], name="faces",
        scratch_shapes=[pltpu.SemaphoreType.DMA],
        compiler_params=pltpu.CompilerParams(vmem_limit_bytes=4 << 20),
        cost_estimate=pl.CostEstimate(flops=4_000_000_000, bytes_accessed=200_000_000, transcendentals=0),
    )(pltpu.with_memory_space_constraint(adj, pltpu.HBM))
    adj = pltpu.with_memory_space_constraint(adj, pltpu.VMEM)
    halos = swap_halos(*sends)
    hbm = [pltpu.with_memory_space_constraint(x, pltpu.HBM) for x in (g, diag, pre)]
    part, *edges, g, diag, pre = first_part(adj, off, *hbm)
    g, diag, pre = [pltpu.with_memory_space_constraint(x, pltpu.VMEM) for x in (g, diag, pre)]
    adj, *sends = halo_part(part, halos, off, pre, edges)
    halos = swap_halos(*sends)
    part = second_part(adj, g, off, diag, pre)
    cell = face_cell.reshape(-1, 128)
    side = face_side.reshape(-1, 128)
    adj, sums = halo_part(part, halos, off, pre, edges, (cell, side, design))
    total = combine(sums)
    nr = lax.axis_size("radax")
    owned = total.shape[1] // nr
    sensitivity = lax.dynamic_slice_in_dim(total, lax.axis_index("radax") * owned, owned, 1)
    return adj.transpose(0, 2, 1, 3), sensitivity


def solution(mesh):
    in_specs = (
        P("circ", "radax", None, None),
        P("circ", "radax", None, None),
        P(None, None, "circ", "radax", None, None),
        P(None, "circ", "radax", None, None),
        P(None, "circ", "radax", None, None),
        P(("circ", "radax")),
        P(("circ", "radax")),
        P(("circ", "radax"), None, None),
    )
    out_specs = (P("circ", "radax", None, None), P("circ", "radax"))
    return jax.shard_map(body, mesh=mesh, in_specs=in_specs, out_specs=out_specs, check_vma=False)
```

```python
import jax
import jax.numpy as jnp
from jax import lax
from jax.experimental import pallas as pl
from jax.experimental.pallas import tpu as pltpu
from jax.sharding import PartitionSpec as P


F32 = jnp.float32
PARAMS = pltpu.CompilerParams(vmem_limit_bytes=28 << 20)


def _vmem():
    return pl.BlockSpec(memory_space=pltpu.VMEM)


def send_faces(adj, even_ref, odd_ref, near_ref, far_ref):
    nt, nv, nq, _ = adj.shape
    c = lax.axis_index("circ")
    r = lax.axis_index("radax")
    t_even = jnp.where(c % 2 == 0, nt - 1, 0)
    even_ref[...] = adj[t_even]
    odd_ref[...] = adj[nt - 1 - t_even]
    up = r % 2 == 0
    for t in range(nt):
        for i in range(nv):
            low = adj[t, i, 0:1, :]
            high = adj[t, i, nq - 1 : nq, :]
            near_ref[i, t : t + 1, :] = jnp.where(up, high, low)
            far_ref[i, t : t + 1, :] = jnp.where(up, low, high)


def faces_kernel(adj_hbm, adj_ref, even_ref, odd_ref, near_ref, far_ref, sem):
    copy = pltpu.make_async_copy(adj_hbm, adj_ref, sem)
    copy.start()
    copy.wait()
    send_faces(adj_ref, even_ref, odd_ref, near_ref, far_ref)


def shift_lanes(plane, step):
    width = plane.shape[1]
    lane = lax.broadcasted_iota(jnp.int32, plane.shape, 1)
    edge = 0 if step == 1 else width - 1
    return jnp.where(lane == edge, 0.0, pltpu.roll(plane, step % width, 1))


def shift_rows(plane, step):
    rows = plane.shape[0]
    row = lax.broadcasted_iota(jnp.int32, plane.shape, 0)
    edge = 0 if step == 1 else rows - 1
    return jnp.where(row == edge, 0.0, pltpu.roll(plane, step % rows, 0))


def keep_row(rows_ref, t, plane, q):
    here = lax.broadcasted_iota(jnp.int32, rows_ref.shape, 0) == t
    pltpu.store(rows_ref, jnp.broadcast_to(plane[q : q + 1, :], rows_ref.shape), mask=here)


def local_layer(t, adj_ref, g_ref, off_ref, diag_ref, pre_ref, out_ref, edge_refs=(), wait=None):
    nt, nv, nq, _ = adj_ref.shape
    below = jnp.maximum(t - 1, 0)
    above = jnp.minimum(t + 1, nt - 1)
    has_below = (t > 0).astype(F32)
    has_above = (t < nt - 1).astype(F32)
    acc = [jnp.zeros(adj_ref.shape[2:], F32)] * nv
    for j in range(nv):
        here = adj_ref[t, j]
        fields = [
            adj_ref[below, j] * has_below,
            adj_ref[above, j] * has_above,
            shift_rows(here, 1),
            shift_rows(here, -1),
            shift_lanes(here, 1),
            shift_lanes(here, -1),
        ]
        for k in range(6):
            for i in range(nv):
                block = off_ref[k, j, t, i].astype(F32)
                acc[i] = acc[i] + block * fields[k]
                if edge_refs and k in (2, 3):
                    keep_row(edge_refs[k - 2].at[j, i], t, block, 0 if k == 2 else nq - 1)
    if wait is not None:
        wait()
    for j in range(nv):
        here = adj_ref[t, j]
        for i in range(nv):
            acc[i] = acc[i] + diag_ref[j, t, i].astype(F32) * here
    acc = [g_ref[t, i] - acc[i] for i in range(nv)]
    new = [adj_ref[t, i] for i in range(nv)]
    for j in range(nv):
        for i in range(nv):
            block = pre_ref[j, t, i].astype(F32)
            new[i] = new[i] + block * acc[j]
            if edge_refs:
                keep_row(edge_refs[2].at[j, i], t, block, 0)
                keep_row(edge_refs[3].at[j, i], t, block, nq - 1)
    for i in range(nv):
        out_ref[t, i] = new[i]


def first_kernel(adj_ref, off_ref, g_hbm, diag_hbm, pre_hbm,
                 out_ref, e0, e1, e2, e3, g_ref, diag_ref, pre_ref, sems):
    nt = adj_ref.shape[0]

    def copies(t):
        return [
            pltpu.make_async_copy(g_hbm.at[t], g_ref.at[t], sems.at[0, t]),
            pltpu.make_async_copy(diag_hbm.at[:, t], diag_ref.at[:, t], sems.at[1, t]),
            pltpu.make_async_copy(pre_hbm.at[:, t], pre_ref.at[:, t], sems.at[2, t]),
        ]

    for t in range(nt):
        for copy in copies(t):
            copy.start()

    def layer(t, carry):
        def wait():
            for copy in copies(t):
                copy.wait()

        local_layer(t, adj_ref, g_ref, off_ref, diag_ref, pre_ref, out_ref, (e0, e1, e2, e3), wait)
        return carry

    lax.fori_loop(0, nt, layer, 0)


def second_kernel(adj_ref, g_ref, off_ref, diag_ref, pre_ref, out_ref):
    def layer(t, carry):
        local_layer(t, adj_ref, g_ref, off_ref, diag_ref, pre_ref, out_ref)
        return carry

    lax.fori_loop(0, adj_ref.shape[0], layer, 0)


COST = pl.CostEstimate(flops=40_000_000, bytes_accessed=24_000_000, transcendentals=0)


def first_part(adj, off, g, diag, pre):
    nt, nv, _, na = adj.shape
    out_shape = [jax.ShapeDtypeStruct(adj.shape, F32)]
    out_shape += [jax.ShapeDtypeStruct((nv, nv, nt, na), F32)] * 4
    out_shape += [pltpu.VMEM(x.shape, x.dtype) for x in (g, diag, pre)]
    return pl.pallas_call(
        first_kernel,
        in_specs=[_vmem()] * 2 + [pl.BlockSpec(memory_space=pltpu.HBM)] * 3,
        out_specs=[_vmem()] * len(out_shape),
        out_shape=out_shape,
        scratch_shapes=[pltpu.SemaphoreType.DMA((3, nt))],
        compiler_params=PARAMS,
        cost_estimate=COST,
        name="local_first",
    )(adj, off, g, diag, pre)


def second_part(adj, g, off, diag, pre):
    return pl.pallas_call(
        second_kernel,
        in_specs=[_vmem()] * 5,
        out_specs=_vmem(),
        out_shape=jax.ShapeDtypeStruct(adj.shape, F32),
        compiler_params=PARAMS,
        cost_estimate=COST,
        name="local_second",
    )(adj, g, off, diag, pre)


def apply_blocks(load, vectors):
    nv = len(vectors)
    out = []
    for i in range(nv):
        total = load(0, i) * vectors[0]
        for j in range(1, nv):
            total = total + load(j, i) * vectors[j]
        out.append(total)
    return out


def add_halos(adj_ref, even, odd, near, far, off_ref, pre_ref, edges, out_ref):
    nt, nv, nq, _ = adj_ref.shape
    c = lax.axis_index("circ")
    r = lax.axis_index("radax")
    c_even = c % 2 == 0
    r_even = r % 2 == 0
    out_ref[...] = adj_ref[...]
    for t, low in ((0, True), (nt - 1, False)):
        k = 0 if low else 1
        pick = jnp.logical_not(c_even) if low else c_even
        halo = [jnp.where(pick, even[j], odd[j]) for j in range(nv)]
        extra = apply_blocks(lambda j, i: off_ref[k, j, t, i].astype(F32), halo)
        change = apply_blocks(lambda j, i: pre_ref[j, t, i].astype(F32), extra)
        for i in range(nv):
            out_ref[t, i] = out_ref[t, i] - change[i]
    last = lax.axis_size("radax") - 1
    for q, low in ((0, True), (nq - 1, False)):
        off, pre = (edges[0], edges[2]) if low else (edges[1], edges[3])
        pick = jnp.logical_not(r_even) if low else r_even
        inside = (r > 0) if low else (r < last)
        halo = [jnp.where(inside, jnp.where(pick, near[j], far[j]), 0.0) for j in range(nv)]
        extra = apply_blocks(lambda j, i: off[j, i], halo)
        change = apply_blocks(lambda j, i: pre[j, i], extra)
        for t in range(nt):
            for i in range(nv):
                out_ref[t, i, q : q + 1, :] = out_ref[t, i, q : q + 1, :] - change[i][t : t + 1, :]


def halo_kernel(adj_ref, even, odd, near, far, off_ref, pre_ref, e0, e1, e2, e3,
                out_ref, even_out, odd_out, near_out, far_out):
    add_halos(adj_ref, even, odd, near, far, off_ref, pre_ref, (e0, e1, e2, e3), out_ref)
    send_faces(out_ref, even_out, odd_out, near_out, far_out)


def final_kernel(adj_ref, even, odd, near, far, off_ref, pre_ref, e0, e1, e2, e3,
                 side_ref, design_ref, cell_ref, out_hbm, sums_ref, out_ref, by_cell, places, table, sems):
    nt, nv, nq, na = adj_ref.shape
    chunks = cell_ref.shape[0]
    cell = cell_ref[...]
    lane = lax.broadcasted_iota(jnp.int32, cell.shape, 1)
    places[0:chunks, :] = (cell >> 7) * 8 + (cell >> (na.bit_length() - 1))
    places[chunks : 2 * chunks, :] = (lane - cell) & 127
    look_up = pltpu.make_async_copy(places, table, sems.at[0])
    look_up.start()
    add_halos(adj_ref, even, odd, near, far, off_ref, pre_ref, (e0, e1, e2, e3), out_ref)
    result = pltpu.make_async_copy(out_ref, out_hbm, sems.at[1])
    result.start()
    halves = na // 128
    pitch = 8 * halves + 1
    for t in range(nt):
        for i in range(nv):
            for qt in range(nq // 8):
                for h in range(halves):
                    first = (t * nq + qt * 8) * pitch + h * 8 + i
                    by_cell[pl.ds(first, 8, stride=pitch), :] = out_ref[
                        t, i, qt * 8 : qt * 8 + 8, h * 128 : h * 128 + 128
                    ]
    lane = lax.broadcasted_iota(jnp.int32, (8, 128), 1)
    field = lax.broadcasted_iota(jnp.int32, (8, 128), 0)
    look_up.wait()

    every = jnp.zeros((8, 128), F32)
    upper = jnp.zeros((8, 128), F32)
    for k in range(chunks):
        side = jnp.broadcast_to(side_ref[k : k + 1, :].astype(F32), (8, 128))
        picked = jnp.zeros((8, 128), F32)
        for f in range(128):
            tile = by_cell[pl.ds(table[k, f], 8), :]
            picked = jnp.where(lane == f, pltpu.roll(tile, table[k + chunks, f], 1), picked)
        by_face = jnp.transpose(jnp.where(field == 6, side, picked))
        contrib = jnp.zeros((128, 128), F32)
        for i in range(nv):
            contrib = contrib + by_face[:, i : i + 1] * design_ref[i, k * 128 : k * 128 + 128, :]
        every = every + jnp.sum(contrib.reshape(16, 8, 128), axis=0)
        upper = upper + jnp.sum((contrib * by_face[:, 6:7]).reshape(16, 8, 128), axis=0)
    upper = jnp.sum(upper, axis=0, keepdims=True)
    sums_ref[0:1, :] = jnp.sum(every, axis=0, keepdims=True) - upper
    sums_ref[1:2, :] = upper
    result.wait()


def halo_part(adj, halos, off, pre, edges, faces=None):
    nt, _, nq, na = adj.shape
    args = [adj, *halos, off, pre, *edges]
    cost = pl.CostEstimate(flops=4_000_000, bytes_accessed=5_000_000, transcendentals=0)
    out_shape = [jax.ShapeDtypeStruct(adj.shape, F32)]
    if faces is None:
        out_shape += [jax.ShapeDtypeStruct(h.shape, F32) for h in halos]
        return pl.pallas_call(
            halo_kernel, in_specs=[_vmem()] * len(args), out_specs=[_vmem()] * 5, out_shape=out_shape,
            compiler_params=PARAMS, cost_estimate=cost, name="halo_first",
        )(*args)
    cell, side, design = faces
    out_shape += [jax.ShapeDtypeStruct((2, design.shape[2]), F32)]
    return pl.pallas_call(
        final_kernel, in_specs=[_vmem()] * (len(args) + 3),
        out_specs=[pl.BlockSpec(memory_space=pltpu.HBM), _vmem()], out_shape=out_shape,
        scratch_shapes=[
            pltpu.VMEM(adj.shape, F32),
            pltpu.VMEM((nt * nq * (na // 16 + 1), 128), F32),
            pltpu.VMEM((2 * cell.shape[0], 128), jnp.int32),
            pltpu.SMEM((2 * cell.shape[0], 128), jnp.int32),
            pltpu.SemaphoreType.DMA((2,)),
        ],
        compiler_params=PARAMS, cost_estimate=cost, name="halo_last",
    )(*args, side, design, cell)


def swap_halos(even, odd, near, far):
    nc = lax.axis_size("circ")
    nr = lax.axis_size("radax")
    odd = lax.ppermute(odd, "circ", [(i, (i + 1) % nc if i % 2 else (i - 1) % nc) for i in range(nc)])
    far = lax.ppermute(far, "radax", [(i, nr - 1 - i) for i in range(nr)])
    even = lax.ppermute(even, "circ", [(i, i ^ 1) for i in range(nc)])
    near = lax.ppermute(near, "radax", [(i, i ^ 1) for i in range(nr)])
    return even, odd, near, far


def combine(sums):
    nc = lax.axis_size("circ")
    nr = lax.axis_size("radax")
    lower, upper = sums[0:1], sums[1:2]

    def ring(flip):
        return [(c * nr + r, (c + 1) % nc * nr + (r ^ flip)) for c in range(nc) for r in range(nr)]

    crossed = lax.ppermute(upper, ("circ", "radax"), ring(2))
    straight = lax.ppermute(upper, ("circ", "radax"), ring(0))
    other = lax.ppermute(lower, "radax", [(i, i ^ 2) for i in range(nr)])
    mine = (lower + other) + (straight + crossed)
    return mine + lax.ppermute(mine, "radax", [(i, i ^ 1) for i in range(nr)])


def body(objective_grad, adjoint_start, jac_off, jac_diag, precond, face_cell, face_side, design_grad):
    g = objective_grad.transpose(0, 2, 1, 3)
    adj = adjoint_start.transpose(0, 2, 1, 3)
    off = jac_off.transpose(0, 1, 2, 4, 3, 5)
    diag = jac_diag.transpose(0, 1, 3, 2, 4)
    pre = precond.transpose(0, 1, 3, 2, 4)
    design = design_grad.transpose(1, 0, 2)
    nt, nv, nq, na = adj.shape
    ring = jax.ShapeDtypeStruct((nv, nq, na), F32)
    rows = jax.ShapeDtypeStruct((nv, nt, na), F32)
    adj, *sends = pl.pallas_call(
        faces_kernel, in_specs=[pl.BlockSpec(memory_space=pltpu.HBM)], out_specs=[_vmem()] * 5,
        out_shape=[pltpu.VMEM(adj.shape, F32), ring, ring, rows, rows], name="faces",
        scratch_shapes=[pltpu.SemaphoreType.DMA],
        compiler_params=pltpu.CompilerParams(vmem_limit_bytes=4 << 20),
        cost_estimate=pl.CostEstimate(flops=4_000_000_000, bytes_accessed=200_000_000, transcendentals=0),
    )(pltpu.with_memory_space_constraint(adj, pltpu.HBM))
    adj = pltpu.with_memory_space_constraint(adj, pltpu.VMEM)
    halos = swap_halos(*sends)
    hbm = [pltpu.with_memory_space_constraint(x, pltpu.HBM) for x in (g, diag, pre)]
    part, *edges, g, diag, pre = first_part(adj, off, *hbm)
    g, diag, pre = [pltpu.with_memory_space_constraint(x, pltpu.VMEM) for x in (g, diag, pre)]
    adj, *sends = halo_part(part, halos, off, pre, edges)
    halos = swap_halos(*sends)
    part = second_part(adj, g, off, diag, pre)
    cell = face_cell.reshape(-1, 128)
    side = face_side.reshape(-1, 128)
    adj, sums = halo_part(part, halos, off, pre, edges, (cell, side, design))
    total = combine(sums)
    nr = lax.axis_size("radax")
    owned = total.shape[1] // nr
    sensitivity = lax.dynamic_slice_in_dim(total, lax.axis_index("radax") * owned, owned, 1)
    return adj.transpose(0, 2, 1, 3), sensitivity


def solution(mesh):
    in_specs = (
        P("circ", "radax", None, None),
        P("circ", "radax", None, None),
        P(None, None, "circ", "radax", None, None),
        P(None, "circ", "radax", None, None),
        P(None, "circ", "radax", None, None),
        P(("circ", "radax")),
        P(("circ", "radax")),
        P(("circ", "radax"), None, None),
    )
    out_specs = (P("circ", "radax", None, None), P("circ", "radax"))
    return jax.shard_map(body, mesh=mesh, in_specs=in_specs, out_specs=out_specs, check_vma=False)
```

```python
import jax
import jax.numpy as jnp
from jax import lax
from jax.experimental import pallas as pl
from jax.experimental.pallas import tpu as pltpu
from jax.sharding import PartitionSpec as P


F32 = jnp.float32
PARAMS = pltpu.CompilerParams(vmem_limit_bytes=28 << 20)


def _vmem():
    return pl.BlockSpec(memory_space=pltpu.VMEM)


def send_faces(adj, even_ref, odd_ref, near_ref, far_ref):
    nt, nv, nq, _ = adj.shape
    c = lax.axis_index("circ")
    r = lax.axis_index("radax")
    t_even = jnp.where(c % 2 == 0, nt - 1, 0)
    even_ref[...] = adj[t_even]
    odd_ref[...] = adj[nt - 1 - t_even]
    up = r % 2 == 0
    for t in range(nt):
        for i in range(nv):
            low = adj[t, i, 0:1, :]
            high = adj[t, i, nq - 1 : nq, :]
            near_ref[i, t : t + 1, :] = jnp.where(up, high, low)
            far_ref[i, t : t + 1, :] = jnp.where(up, low, high)


def faces_kernel(adj_hbm, adj_ref, even_ref, odd_ref, near_ref, far_ref, sem):
    copy = pltpu.make_async_copy(adj_hbm, adj_ref, sem)
    copy.start()
    copy.wait()
    send_faces(adj_ref, even_ref, odd_ref, near_ref, far_ref)


def shift_lanes(plane, step):
    width = plane.shape[1]
    lane = lax.broadcasted_iota(jnp.int32, plane.shape, 1)
    edge = 0 if step == 1 else width - 1
    return jnp.where(lane == edge, 0.0, pltpu.roll(plane, step % width, 1))


def shift_rows(plane, step):
    rows = plane.shape[0]
    row = lax.broadcasted_iota(jnp.int32, plane.shape, 0)
    edge = 0 if step == 1 else rows - 1
    return jnp.where(row == edge, 0.0, pltpu.roll(plane, step % rows, 0))


def keep_row(rows_ref, t, plane, q):
    here = lax.broadcasted_iota(jnp.int32, rows_ref.shape, 0) == t
    pltpu.store(rows_ref, jnp.broadcast_to(plane[q : q + 1, :], rows_ref.shape), mask=here)


def local_layer(t, adj_ref, g_ref, off_ref, diag_ref, pre_ref, out_ref, edge_refs=(), wait=None):
    nt, nv, nq, _ = adj_ref.shape
    below = jnp.maximum(t - 1, 0)
    above = jnp.minimum(t + 1, nt - 1)
    has_below = (t > 0).astype(F32)
    has_above = (t < nt - 1).astype(F32)
    acc = [jnp.zeros(adj_ref.shape[2:], F32)] * nv
    for j in range(nv):
        here = adj_ref[t, j]
        fields = [
            adj_ref[below, j] * has_below,
            adj_ref[above, j] * has_above,
            shift_rows(here, 1),
            shift_rows(here, -1),
            shift_lanes(here, 1),
            shift_lanes(here, -1),
        ]
        for k in range(6):
            for i in range(nv):
                block = off_ref[k, j, t, i].astype(F32)
                acc[i] = acc[i] + block * fields[k]
                if edge_refs and k in (2, 3):
                    keep_row(edge_refs[k - 2].at[j, i], t, block, 0 if k == 2 else nq - 1)
    if wait is not None:
        wait()
    for j in range(nv):
        here = adj_ref[t, j]
        for i in range(nv):
            acc[i] = acc[i] + diag_ref[j, t, i].astype(F32) * here
    acc = [g_ref[t, i] - acc[i] for i in range(nv)]
    new = [adj_ref[t, i] for i in range(nv)]
    for j in range(nv):
        for i in range(nv):
            block = pre_ref[j, t, i].astype(F32)
            new[i] = new[i] + block * acc[j]
            if edge_refs:
                keep_row(edge_refs[2].at[j, i], t, block, 0)
                keep_row(edge_refs[3].at[j, i], t, block, nq - 1)
    for i in range(nv):
        out_ref[t, i] = new[i]


def first_kernel(adj_ref, off_ref, g_hbm, diag_hbm, pre_hbm,
                 out_ref, e0, e1, e2, e3, g_ref, diag_ref, pre_ref, sems):
    nt = adj_ref.shape[0]

    def copies(t):
        return [
            pltpu.make_async_copy(g_hbm.at[t], g_ref.at[t], sems.at[0, t]),
            pltpu.make_async_copy(diag_hbm.at[:, t], diag_ref.at[:, t], sems.at[1, t]),
            pltpu.make_async_copy(pre_hbm.at[:, t], pre_ref.at[:, t], sems.at[2, t]),
        ]

    for t in range(nt):
        for copy in copies(t):
            copy.start()

    def layer(t, carry):
        def wait():
            for copy in copies(t):
                copy.wait()

        local_layer(t, adj_ref, g_ref, off_ref, diag_ref, pre_ref, out_ref, (e0, e1, e2, e3), wait)
        return carry

    lax.fori_loop(0, nt, layer, 0)


def second_kernel(adj_ref, g_ref, off_ref, diag_ref, pre_ref, out_ref):
    def layer(t, carry):
        local_layer(t, adj_ref, g_ref, off_ref, diag_ref, pre_ref, out_ref)
        return carry

    lax.fori_loop(0, adj_ref.shape[0], layer, 0)


COST = pl.CostEstimate(flops=40_000_000, bytes_accessed=24_000_000, transcendentals=0)


def first_part(adj, off, g, diag, pre):
    nt, nv, _, na = adj.shape
    out_shape = [jax.ShapeDtypeStruct(adj.shape, F32)]
    out_shape += [jax.ShapeDtypeStruct((nv, nv, nt, na), F32)] * 4
    out_shape += [pltpu.VMEM(x.shape, x.dtype) for x in (g, diag, pre)]
    return pl.pallas_call(
        first_kernel,
        in_specs=[_vmem()] * 2 + [pl.BlockSpec(memory_space=pltpu.HBM)] * 3,
        out_specs=[_vmem()] * len(out_shape),
        out_shape=out_shape,
        scratch_shapes=[pltpu.SemaphoreType.DMA((3, nt))],
        compiler_params=PARAMS,
        cost_estimate=COST,
        name="local_first",
    )(adj, off, g, diag, pre)


def second_part(adj, g, off, diag, pre):
    return pl.pallas_call(
        second_kernel,
        in_specs=[_vmem()] * 5,
        out_specs=_vmem(),
        out_shape=jax.ShapeDtypeStruct(adj.shape, F32),
        compiler_params=PARAMS,
        cost_estimate=COST,
        name="local_second",
    )(adj, g, off, diag, pre)


def apply_blocks(load, vectors):
    nv = len(vectors)
    out = []
    for i in range(nv):
        total = load(0, i) * vectors[0]
        for j in range(1, nv):
            total = total + load(j, i) * vectors[j]
        out.append(total)
    return out


def add_halos(adj_ref, even, odd, near, far, off_ref, pre_ref, edges, out_ref):
    nt, nv, nq, _ = adj_ref.shape
    c = lax.axis_index("circ")
    r = lax.axis_index("radax")
    c_even = c % 2 == 0
    r_even = r % 2 == 0
    out_ref[...] = adj_ref[...]
    for t, low in ((0, True), (nt - 1, False)):
        k = 0 if low else 1
        pick = jnp.logical_not(c_even) if low else c_even
        halo = [jnp.where(pick, even[j], odd[j]) for j in range(nv)]
        extra = apply_blocks(lambda j, i: off_ref[k, j, t, i].astype(F32), halo)
        change = apply_blocks(lambda j, i: pre_ref[j, t, i].astype(F32), extra)
        for i in range(nv):
            out_ref[t, i] = out_ref[t, i] - change[i]
    last = lax.axis_size("radax") - 1
    for q, low in ((0, True), (nq - 1, False)):
        off, pre = (edges[0], edges[2]) if low else (edges[1], edges[3])
        pick = jnp.logical_not(r_even) if low else r_even
        inside = (r > 0) if low else (r < last)
        halo = [jnp.where(inside, jnp.where(pick, near[j], far[j]), 0.0) for j in range(nv)]
        extra = apply_blocks(lambda j, i: off[j, i], halo)
        change = apply_blocks(lambda j, i: pre[j, i], extra)
        for t in range(nt):
            for i in range(nv):
                out_ref[t, i, q : q + 1, :] = out_ref[t, i, q : q + 1, :] - change[i][t : t + 1, :]


def halo_kernel(adj_ref, even, odd, near, far, off_ref, pre_ref, e0, e1, e2, e3,
                out_ref, even_out, odd_out, near_out, far_out):
    add_halos(adj_ref, even, odd, near, far, off_ref, pre_ref, (e0, e1, e2, e3), out_ref)
    send_faces(out_ref, even_out, odd_out, near_out, far_out)


def final_kernel(adj_ref, even, odd, near, far, off_ref, pre_ref, e0, e1, e2, e3,
                 side_ref, design_ref, cell_ref, out_hbm, sums_ref, out_ref, by_cell, places, table, sems):
    nt, nv, nq, na = adj_ref.shape
    chunks = cell_ref.shape[0]
    cell = cell_ref[...]
    lane = lax.broadcasted_iota(jnp.int32, cell.shape, 1)
    places[0:chunks, :] = (cell >> 7) * 8 + (cell >> (na.bit_length() - 1))
    places[chunks : 2 * chunks, :] = (lane - cell) & 127
    look_up = pltpu.make_async_copy(places, table, sems.at[0])
    look_up.start()
    add_halos(adj_ref, even, odd, near, far, off_ref, pre_ref, (e0, e1, e2, e3), out_ref)
    result = pltpu.make_async_copy(out_ref, out_hbm, sems.at[1])
    result.start()
    halves = na // 128
    pitch = 8 * halves + 1
    for t in range(nt):
        for i in range(nv):
            for qt in range(nq // 8):
                for h in range(halves):
                    first = (t * nq + qt * 8) * pitch + h * 8 + i
                    by_cell[pl.ds(first, 8, stride=pitch), :] = out_ref[
                        t, i, qt * 8 : qt * 8 + 8, h * 128 : h * 128 + 128
                    ]
    lane = lax.broadcasted_iota(jnp.int32, (8, 128), 1)
    field = lax.broadcasted_iota(jnp.int32, (8, 128), 0)
    look_up.wait()

    picked = [jnp.zeros((8, 128), F32)] * chunks
    for f in range(128):
        place = lane == f
        for k in range(chunks):
            tile = by_cell[pl.ds(table[k, f], 8), :]
            picked[k] = jnp.where(place, pltpu.roll(tile, table[k + chunks, f], 1), picked[k])
    every = jnp.zeros((8, 128), F32)
    upper = jnp.zeros((8, 128), F32)
    for k in range(chunks):
        side = jnp.broadcast_to(side_ref[k : k + 1, :].astype(F32), (8, 128))
        by_face = jnp.transpose(jnp.where(field == 6, side, picked[k]))
        contrib = jnp.zeros((128, 128), F32)
        for i in range(nv):
            contrib = contrib + by_face[:, i : i + 1] * design_ref[i, k * 128 : k * 128 + 128, :]
        every = every + jnp.sum(contrib.reshape(16, 8, 128), axis=0)
        upper = upper + jnp.sum((contrib * by_face[:, 6:7]).reshape(16, 8, 128), axis=0)
    upper = jnp.sum(upper, axis=0, keepdims=True)
    sums_ref[0:1, :] = jnp.sum(every, axis=0, keepdims=True) - upper
    sums_ref[1:2, :] = upper
    result.wait()


def halo_part(adj, halos, off, pre, edges, faces=None):
    nt, _, nq, na = adj.shape
    args = [adj, *halos, off, pre, *edges]
    cost = pl.CostEstimate(flops=4_000_000, bytes_accessed=5_000_000, transcendentals=0)
    out_shape = [jax.ShapeDtypeStruct(adj.shape, F32)]
    if faces is None:
        out_shape += [jax.ShapeDtypeStruct(h.shape, F32) for h in halos]
        return pl.pallas_call(
            halo_kernel, in_specs=[_vmem()] * len(args), out_specs=[_vmem()] * 5, out_shape=out_shape,
            compiler_params=PARAMS, cost_estimate=cost, name="halo_first",
        )(*args)
    cell, side, design = faces
    out_shape += [jax.ShapeDtypeStruct((2, design.shape[2]), F32)]
    return pl.pallas_call(
        final_kernel, in_specs=[_vmem()] * (len(args) + 3),
        out_specs=[pl.BlockSpec(memory_space=pltpu.HBM), _vmem()], out_shape=out_shape,
        scratch_shapes=[
            pltpu.VMEM(adj.shape, F32),
            pltpu.VMEM((nt * nq * (na // 16 + 1), 128), F32),
            pltpu.VMEM((2 * cell.shape[0], 128), jnp.int32),
            pltpu.SMEM((2 * cell.shape[0], 128), jnp.int32),
            pltpu.SemaphoreType.DMA((2,)),
        ],
        compiler_params=PARAMS, cost_estimate=cost, name="halo_last",
    )(*args, side, design, cell)


def swap_halos(even, odd, near, far):
    nc = lax.axis_size("circ")
    nr = lax.axis_size("radax")
    odd = lax.ppermute(odd, "circ", [(i, (i + 1) % nc if i % 2 else (i - 1) % nc) for i in range(nc)])
    far = lax.ppermute(far, "radax", [(i, nr - 1 - i) for i in range(nr)])
    even = lax.ppermute(even, "circ", [(i, i ^ 1) for i in range(nc)])
    near = lax.ppermute(near, "radax", [(i, i ^ 1) for i in range(nr)])
    return even, odd, near, far


def combine(sums):
    nc = lax.axis_size("circ")
    nr = lax.axis_size("radax")
    lower, upper = sums[0:1], sums[1:2]

    def ring(flip):
        return [(c * nr + r, (c + 1) % nc * nr + (r ^ flip)) for c in range(nc) for r in range(nr)]

    crossed = lax.ppermute(upper, ("circ", "radax"), ring(2))
    straight = lax.ppermute(upper, ("circ", "radax"), ring(0))
    other = lax.ppermute(lower, "radax", [(i, i ^ 2) for i in range(nr)])
    mine = (lower + other) + (straight + crossed)
    return mine + lax.ppermute(mine, "radax", [(i, i ^ 1) for i in range(nr)])


def body(objective_grad, adjoint_start, jac_off, jac_diag, precond, face_cell, face_side, design_grad):
    g = objective_grad.transpose(0, 2, 1, 3)
    adj = adjoint_start.transpose(0, 2, 1, 3)
    off = jac_off.transpose(0, 1, 2, 4, 3, 5)
    diag = jac_diag.transpose(0, 1, 3, 2, 4)
    pre = precond.transpose(0, 1, 3, 2, 4)
    design = design_grad.transpose(1, 0, 2)
    nt, nv, nq, na = adj.shape
    ring = jax.ShapeDtypeStruct((nv, nq, na), F32)
    rows = jax.ShapeDtypeStruct((nv, nt, na), F32)
    adj, *sends = pl.pallas_call(
        faces_kernel, in_specs=[pl.BlockSpec(memory_space=pltpu.HBM)], out_specs=[_vmem()] * 5,
        out_shape=[pltpu.VMEM(adj.shape, F32), ring, ring, rows, rows], name="faces",
        scratch_shapes=[pltpu.SemaphoreType.DMA],
        compiler_params=pltpu.CompilerParams(vmem_limit_bytes=4 << 20),
        cost_estimate=pl.CostEstimate(flops=4_000_000_000, bytes_accessed=200_000_000, transcendentals=0),
    )(pltpu.with_memory_space_constraint(adj, pltpu.HBM))
    adj = pltpu.with_memory_space_constraint(adj, pltpu.VMEM)
    halos = swap_halos(*sends)
    hbm = [pltpu.with_memory_space_constraint(x, pltpu.HBM) for x in (g, diag, pre)]
    part, *edges, g, diag, pre = first_part(adj, off, *hbm)
    g, diag, pre = [pltpu.with_memory_space_constraint(x, pltpu.VMEM) for x in (g, diag, pre)]
    adj, *sends = halo_part(part, halos, off, pre, edges)
    halos = swap_halos(*sends)
    part = second_part(adj, g, off, diag, pre)
    cell = face_cell.reshape(-1, 128)
    side = face_side.reshape(-1, 128)
    adj, sums = halo_part(part, halos, off, pre, edges, (cell, side, design))
    total = combine(sums)
    nr = lax.axis_size("radax")
    owned = total.shape[1] // nr
    sensitivity = lax.dynamic_slice_in_dim(total, lax.axis_index("radax") * owned, owned, 1)
    return adj.transpose(0, 2, 1, 3), sensitivity


def solution(mesh):
    in_specs = (
        P("circ", "radax", None, None),
        P("circ", "radax", None, None),
        P(None, None, "circ", "radax", None, None),
        P(None, "circ", "radax", None, None),
        P(None, "circ", "radax", None, None),
        P(("circ", "radax")),
        P(("circ", "radax")),
        P(("circ", "radax"), None, None),
    )
    out_specs = (P("circ", "radax", None, None), P("circ", "radax"))
    return jax.shard_map(body, mesh=mesh, in_specs=in_specs, out_specs=out_specs, check_vma=False)
```

```python
import jax
import jax.numpy as jnp
from jax import lax
from jax.experimental import pallas as pl
from jax.experimental.pallas import tpu as pltpu
from jax.sharding import PartitionSpec as P


F32 = jnp.float32
PARAMS = pltpu.CompilerParams(vmem_limit_bytes=28 << 20)


def _vmem():
    return pl.BlockSpec(memory_space=pltpu.VMEM)


def send_faces(adj, even_ref, odd_ref, near_ref, far_ref):
    nt, nv, nq, _ = adj.shape
    c = lax.axis_index("circ")
    r = lax.axis_index("radax")
    t_even = jnp.where(c % 2 == 0, nt - 1, 0)
    even_ref[...] = adj[t_even]
    odd_ref[...] = adj[nt - 1 - t_even]
    up = r % 2 == 0
    for t in range(nt):
        for i in range(nv):
            low = adj[t, i, 0:1, :]
            high = adj[t, i, nq - 1 : nq, :]
            near_ref[i, t : t + 1, :] = jnp.where(up, high, low)
            far_ref[i, t : t + 1, :] = jnp.where(up, low, high)


def faces_kernel(adj_hbm, adj_ref, even_ref, odd_ref, near_ref, far_ref, sem):
    copy = pltpu.make_async_copy(adj_hbm, adj_ref, sem)
    copy.start()
    copy.wait()
    send_faces(adj_ref, even_ref, odd_ref, near_ref, far_ref)


def shift_lanes(plane, step):
    width = plane.shape[1]
    lane = lax.broadcasted_iota(jnp.int32, plane.shape, 1)
    edge = 0 if step == 1 else width - 1
    return jnp.where(lane == edge, 0.0, pltpu.roll(plane, step % width, 1))


def shift_rows(plane, step):
    rows = plane.shape[0]
    row = lax.broadcasted_iota(jnp.int32, plane.shape, 0)
    edge = 0 if step == 1 else rows - 1
    return jnp.where(row == edge, 0.0, pltpu.roll(plane, step % rows, 0))


def keep_row(rows_ref, t, plane, q):
    here = lax.broadcasted_iota(jnp.int32, rows_ref.shape, 0) == t
    pltpu.store(rows_ref, jnp.broadcast_to(plane[q : q + 1, :], rows_ref.shape), mask=here)


def local_layer(t, adj_ref, g_ref, off_ref, diag_ref, pre_ref, out_ref, edge_refs=(), wait=None):
    nt, nv, nq, _ = adj_ref.shape
    below = jnp.maximum(t - 1, 0)
    above = jnp.minimum(t + 1, nt - 1)
    has_below = (t > 0).astype(F32)
    has_above = (t < nt - 1).astype(F32)
    acc = [None] * nv
    for j in range(nv):
        here = adj_ref[t, j]
        fields = [
            adj_ref[below, j] * has_below,
            adj_ref[above, j] * has_above,
            shift_rows(here, 1),
            shift_rows(here, -1),
            shift_lanes(here, 1),
            shift_lanes(here, -1),
        ]
        for k in range(6):
            for i in range(nv):
                block = off_ref[k, j, t, i].astype(F32)
                term = block * fields[k]
                acc[i] = term if acc[i] is None else acc[i] + term
                if edge_refs and k in (2, 3):
                    keep_row(edge_refs[k - 2].at[j, i], t, block, 0 if k == 2 else nq - 1)
    if wait is not None:
        wait()
    for j in range(nv):
        here = adj_ref[t, j]
        for i in range(nv):
            acc[i] = acc[i] + diag_ref[j, t, i].astype(F32) * here
    acc = [g_ref[t, i] - acc[i] for i in range(nv)]
    new = [adj_ref[t, i] for i in range(nv)]
    for j in range(nv):
        for i in range(nv):
            block = pre_ref[j, t, i].astype(F32)
            new[i] = new[i] + block * acc[j]
            if edge_refs:
                keep_row(edge_refs[2].at[j, i], t, block, 0)
                keep_row(edge_refs[3].at[j, i], t, block, nq - 1)
    for i in range(nv):
        out_ref[t, i] = new[i]


def first_kernel(adj_ref, off_ref, g_hbm, diag_hbm, pre_hbm,
                 out_ref, e0, e1, e2, e3, g_ref, diag_ref, pre_ref, sems):
    nt = adj_ref.shape[0]

    def copies(t):
        return [
            pltpu.make_async_copy(g_hbm.at[t], g_ref.at[t], sems.at[0, t]),
            pltpu.make_async_copy(diag_hbm.at[:, t], diag_ref.at[:, t], sems.at[1, t]),
            pltpu.make_async_copy(pre_hbm.at[:, t], pre_ref.at[:, t], sems.at[2, t]),
        ]

    for t in range(nt):
        for copy in copies(t):
            copy.start()

    def layer(t, carry):
        def wait():
            for copy in copies(t):
                copy.wait()

        local_layer(t, adj_ref, g_ref, off_ref, diag_ref, pre_ref, out_ref, (e0, e1, e2, e3), wait)
        return carry

    lax.fori_loop(0, nt, layer, 0)


def second_kernel(adj_ref, g_ref, off_ref, diag_ref, pre_ref, out_ref):
    def layer(t, carry):
        local_layer(t, adj_ref, g_ref, off_ref, diag_ref, pre_ref, out_ref)
        return carry

    lax.fori_loop(0, adj_ref.shape[0], layer, 0)


COST = pl.CostEstimate(flops=40_000_000, bytes_accessed=24_000_000, transcendentals=0)


def first_part(adj, off, g, diag, pre):
    nt, nv, _, na = adj.shape
    out_shape = [jax.ShapeDtypeStruct(adj.shape, F32)]
    out_shape += [jax.ShapeDtypeStruct((nv, nv, nt, na), F32)] * 4
    out_shape += [pltpu.VMEM(x.shape, x.dtype) for x in (g, diag, pre)]
    return pl.pallas_call(
        first_kernel,
        in_specs=[_vmem()] * 2 + [pl.BlockSpec(memory_space=pltpu.HBM)] * 3,
        out_specs=[_vmem()] * len(out_shape),
        out_shape=out_shape,
        scratch_shapes=[pltpu.SemaphoreType.DMA((3, nt))],
        compiler_params=PARAMS,
        cost_estimate=COST,
        name="local_first",
    )(adj, off, g, diag, pre)


def second_part(adj, g, off, diag, pre):
    return pl.pallas_call(
        second_kernel,
        in_specs=[_vmem()] * 5,
        out_specs=_vmem(),
        out_shape=jax.ShapeDtypeStruct(adj.shape, F32),
        compiler_params=PARAMS,
        cost_estimate=COST,
        name="local_second",
    )(adj, g, off, diag, pre)


def apply_blocks(load, vectors):
    nv = len(vectors)
    out = []
    for i in range(nv):
        total = load(0, i) * vectors[0]
        for j in range(1, nv):
            total = total + load(j, i) * vectors[j]
        out.append(total)
    return out


def add_halos(adj_ref, even, odd, near, far, off_ref, pre_ref, edges, out_ref):
    nt, nv, nq, _ = adj_ref.shape
    c = lax.axis_index("circ")
    r = lax.axis_index("radax")
    c_even = c % 2 == 0
    r_even = r % 2 == 0
    out_ref[...] = adj_ref[...]
    for t, low in ((0, True), (nt - 1, False)):
        k = 0 if low else 1
        pick = jnp.logical_not(c_even) if low else c_even
        halo = [jnp.where(pick, even[j], odd[j]) for j in range(nv)]
        extra = apply_blocks(lambda j, i: off_ref[k, j, t, i].astype(F32), halo)
        change = apply_blocks(lambda j, i: pre_ref[j, t, i].astype(F32), extra)
        for i in range(nv):
            out_ref[t, i] = out_ref[t, i] - change[i]
    last = lax.axis_size("radax") - 1
    for q, low in ((0, True), (nq - 1, False)):
        off, pre = (edges[0], edges[2]) if low else (edges[1], edges[3])
        pick = jnp.logical_not(r_even) if low else r_even
        inside = (r > 0) if low else (r < last)
        halo = [jnp.where(inside, jnp.where(pick, near[j], far[j]), 0.0) for j in range(nv)]
        extra = apply_blocks(lambda j, i: off[j, i], halo)
        change = apply_blocks(lambda j, i: pre[j, i], extra)
        for t in range(nt):
            for i in range(nv):
                out_ref[t, i, q : q + 1, :] = out_ref[t, i, q : q + 1, :] - change[i][t : t + 1, :]


def halo_kernel(adj_ref, even, odd, near, far, off_ref, pre_ref, e0, e1, e2, e3,
                out_ref, even_out, odd_out, near_out, far_out):
    add_halos(adj_ref, even, odd, near, far, off_ref, pre_ref, (e0, e1, e2, e3), out_ref)
    send_faces(out_ref, even_out, odd_out, near_out, far_out)


def final_kernel(adj_ref, even, odd, near, far, off_ref, pre_ref, e0, e1, e2, e3,
                 side_ref, design_ref, cell_ref, out_hbm, sums_ref, out_ref, by_cell, places, table, sems):
    nt, nv, nq, na = adj_ref.shape
    chunks = cell_ref.shape[0]
    cell = cell_ref[...]
    lane = lax.broadcasted_iota(jnp.int32, cell.shape, 1)
    places[0:chunks, :] = (cell >> 7) * 8 + (cell >> (na.bit_length() - 1))
    places[chunks : 2 * chunks, :] = (lane - cell) & 127
    look_up = pltpu.make_async_copy(places, table, sems.at[0])
    look_up.start()
    add_halos(adj_ref, even, odd, near, far, off_ref, pre_ref, (e0, e1, e2, e3), out_ref)
    result = pltpu.make_async_copy(out_ref, out_hbm, sems.at[1])
    result.start()
    halves = na // 128
    pitch = 8 * halves + 1
    for t in range(nt):
        for i in range(nv):
            for qt in range(nq // 8):
                for h in range(halves):
                    first = (t * nq + qt * 8) * pitch + h * 8 + i
                    by_cell[pl.ds(first, 8, stride=pitch), :] = out_ref[
                        t, i, qt * 8 : qt * 8 + 8, h * 128 : h * 128 + 128
                    ]
    lane = lax.broadcasted_iota(jnp.int32, (8, 128), 1)
    field = lax.broadcasted_iota(jnp.int32, (8, 128), 0)
    look_up.wait()

    picked = [jnp.zeros((8, 128), F32)] * chunks
    for f in range(128):
        place = lane == f
        for k in range(chunks):
            tile = by_cell[pl.ds(table[k, f], 8), :]
            picked[k] = jnp.where(place, pltpu.roll(tile, table[k + chunks, f], 1), picked[k])
    every = jnp.zeros((8, 128), F32)
    upper = jnp.zeros((8, 128), F32)
    for k in range(chunks):
        side = jnp.broadcast_to(side_ref[k : k + 1, :].astype(F32), (8, 128))
        by_face = jnp.transpose(jnp.where(field == 6, side, picked[k]))
        contrib = jnp.zeros((128, 128), F32)
        for i in range(nv):
            contrib = contrib + by_face[:, i : i + 1] * design_ref[i, k * 128 : k * 128 + 128, :]
        every = every + jnp.sum(contrib.reshape(16, 8, 128), axis=0)
        upper = upper + jnp.sum((contrib * by_face[:, 6:7]).reshape(16, 8, 128), axis=0)
    upper = jnp.sum(upper, axis=0, keepdims=True)
    sums_ref[0:1, :] = jnp.sum(every, axis=0, keepdims=True) - upper
    sums_ref[1:2, :] = upper
    result.wait()


def halo_part(adj, halos, off, pre, edges, faces=None):
    nt, _, nq, na = adj.shape
    args = [adj, *halos, off, pre, *edges]
    cost = pl.CostEstimate(flops=4_000_000, bytes_accessed=5_000_000, transcendentals=0)
    out_shape = [jax.ShapeDtypeStruct(adj.shape, F32)]
    if faces is None:
        out_shape += [jax.ShapeDtypeStruct(h.shape, F32) for h in halos]
        return pl.pallas_call(
            halo_kernel, in_specs=[_vmem()] * len(args), out_specs=[_vmem()] * 5, out_shape=out_shape,
            compiler_params=PARAMS, cost_estimate=cost, name="halo_first",
        )(*args)
    cell, side, design = faces
    out_shape += [jax.ShapeDtypeStruct((2, design.shape[2]), F32)]
    return pl.pallas_call(
        final_kernel, in_specs=[_vmem()] * (len(args) + 3),
        out_specs=[pl.BlockSpec(memory_space=pltpu.HBM), _vmem()], out_shape=out_shape,
        scratch_shapes=[
            pltpu.VMEM(adj.shape, F32),
            pltpu.VMEM(((nt * nq + 8) * (na // 16 + 1), 128), F32),
            pltpu.VMEM((2 * cell.shape[0], 128), jnp.int32),
            pltpu.SMEM((2 * cell.shape[0], 128), jnp.int32),
            pltpu.SemaphoreType.DMA((2,)),
        ],
        compiler_params=PARAMS, cost_estimate=cost, name="halo_last",
    )(*args, side, design, cell)


def swap_halos(even, odd, near, far):
    nc = lax.axis_size("circ")
    nr = lax.axis_size("radax")
    odd = lax.ppermute(odd, "circ", [(i, (i + 1) % nc if i % 2 else (i - 1) % nc) for i in range(nc)])
    far = lax.ppermute(far, "radax", [(i, nr - 1 - i) for i in range(nr)])
    even = lax.ppermute(even, "circ", [(i, i ^ 1) for i in range(nc)])
    near = lax.ppermute(near, "radax", [(i, i ^ 1) for i in range(nr)])
    return even, odd, near, far


def combine(sums):
    nc = lax.axis_size("circ")
    nr = lax.axis_size("radax")
    lower, upper = sums[0:1], sums[1:2]

    def ring(flip):
        return [(c * nr + r, (c + 1) % nc * nr + (r ^ flip)) for c in range(nc) for r in range(nr)]

    crossed = lax.ppermute(upper, ("circ", "radax"), ring(2))
    straight = lax.ppermute(upper, ("circ", "radax"), ring(0))
    other = lax.ppermute(lower, "radax", [(i, i ^ 2) for i in range(nr)])
    mine = (lower + other) + (straight + crossed)
    return mine + lax.ppermute(mine, "radax", [(i, i ^ 1) for i in range(nr)])


def body(objective_grad, adjoint_start, jac_off, jac_diag, precond, face_cell, face_side, design_grad):
    g = objective_grad.transpose(0, 2, 1, 3)
    adj = adjoint_start.transpose(0, 2, 1, 3)
    off = jac_off.transpose(0, 1, 2, 4, 3, 5)
    diag = jac_diag.transpose(0, 1, 3, 2, 4)
    pre = precond.transpose(0, 1, 3, 2, 4)
    design = design_grad.transpose(1, 0, 2)
    nt, nv, nq, na = adj.shape
    ring = jax.ShapeDtypeStruct((nv, nq, na), F32)
    rows = jax.ShapeDtypeStruct((nv, nt, na), F32)
    adj, *sends = pl.pallas_call(
        faces_kernel, in_specs=[pl.BlockSpec(memory_space=pltpu.HBM)], out_specs=[_vmem()] * 5,
        out_shape=[pltpu.VMEM(adj.shape, F32), ring, ring, rows, rows], name="faces",
        scratch_shapes=[pltpu.SemaphoreType.DMA],
        compiler_params=pltpu.CompilerParams(vmem_limit_bytes=4 << 20),
        cost_estimate=pl.CostEstimate(flops=4_000_000_000, bytes_accessed=200_000_000, transcendentals=0),
    )(pltpu.with_memory_space_constraint(adj, pltpu.HBM))
    adj = pltpu.with_memory_space_constraint(adj, pltpu.VMEM)
    halos = swap_halos(*sends)
    hbm = [pltpu.with_memory_space_constraint(x, pltpu.HBM) for x in (g, diag, pre)]
    part, *edges, g, diag, pre = first_part(adj, off, *hbm)
    g, diag, pre = [pltpu.with_memory_space_constraint(x, pltpu.VMEM) for x in (g, diag, pre)]
    adj, *sends = halo_part(part, halos, off, pre, edges)
    halos = swap_halos(*sends)
    part = second_part(adj, g, off, diag, pre)
    cell = face_cell.reshape(-1, 128)
    side = face_side.reshape(-1, 128)
    adj, sums = halo_part(part, halos, off, pre, edges, (cell, side, design))
    total = combine(sums)
    nr = lax.axis_size("radax")
    owned = total.shape[1] // nr
    sensitivity = lax.dynamic_slice_in_dim(total, lax.axis_index("radax") * owned, owned, 1)
    return adj.transpose(0, 2, 1, 3), sensitivity


def solution(mesh):
    in_specs = (
        P("circ", "radax", None, None),
        P("circ", "radax", None, None),
        P(None, None, "circ", "radax", None, None),
        P(None, "circ", "radax", None, None),
        P(None, "circ", "radax", None, None),
        P(("circ", "radax")),
        P(("circ", "radax")),
        P(("circ", "radax"), None, None),
    )
    out_specs = (P("circ", "radax", None, None), P("circ", "radax"))
    return jax.shard_map(body, mesh=mesh, in_specs=in_specs, out_specs=out_specs, check_vma=False)
```
